512 devices in a mesh: stream: 4 (over z_lo), span: 8 (over z_hi, x), wall: 16 (over y, core).
Axes of the slice: x: 4, y: 8, z: 8 (z_hi: 2, z_lo: 4; z = z_hi * 4 + z_lo), core: 2. Of those that a mesh axis runs over, the one named last changes fastest.
Arguments:
- adj_init: float32 [17, 48, 128, 1024], P(None, 'stream', 'wall', 'span'), may hold values from -1.2 to 1.2
- adj_source: float32 [17, 48, 128, 1024], P(None, 'stream', 'wall', 'span'), may hold values from -12 to 12
- velocity: float32 [3, 48, 128, 1024], P(None, 'stream', 'wall', 'span'), may hold values from -4 to 4
- sound: float32 [48, 128, 1024], P('stream', 'wall', 'span'), may hold values from 0.5 to 2
- face_couple: float32 [3, 2, 17, 17], replicated, may hold values from -0.36 to 0.36
- precond_inv: float32 [17, 17], replicated, may hold values from -0.3 to 1.3
- wall_code: int32 [48, 1024], replicated, may hold values from 0 to 3
- spall_mask: int32 [48, 1024], replicated, may hold values 0 or 1
- wall_table: float32 [4, 17], replicated, may hold values from 0.5 to 2
- spall_gain: float32 [17], replicated, may hold values from 0.5 to 3
Outputs:
- adjoint_out: float32 [17, 48, 128, 1024], P(None, 'stream', 'wall', 'span')
- residual_out: float32 [17, 48, 128, 1024], P(None, 'stream', 'wall', 'span')
The draws below stay inside these ranges and needn't reach their ends.
All inputs are finite; a program needn't handle non-finite values.
Results may differ from the reference program's by a relative error of at most 0.00015.
Values sent between devices are 32-bit elements; how exact they have to be, the bound alone decides.
A program may use at most 128 MiB of HBM per device.

```python
import math
import jax
import jax.numpy as jnp
from jax import lax

NV = 17
KINDS = 4
SWEEPS = 2
NX = 48
NW = 128
NS = 1024


def draw_precond_inv(key, part):
    first_key, second_key = jax.random.split(key)
    row_ids = jnp.arange(NV)
    identity = (row_ids[:, None] == row_ids[None, :]).astype(jnp.float32)
    diagonal_part = jax.random.uniform(first_key, (NV, NV), jnp.float32, 0.7, 1.3)
    off_part = jnp.clip(0.08 * jax.random.normal(second_key, (NV, NV), jnp.float32), -0.3, 0.3)
    return identity * diagonal_part + (1.0 - identity) * off_part


def touch_ends(entries, stream_key, low, high):
    longest = entries.shape.index(max(entries.shape))
    spots = []
    for shift in (0, 1):
        where = [jax.random.randint(jax.random.fold_in(stream_key, axis), (), 0, length) for axis, length in enumerate(entries.shape)]
        where[longest] = (where[longest] + shift) % entries.shape[longest]
        spots.append(tuple(where))
    return entries.at[spots[0]].set(low).at[spots[1]].set(high)


def levels(rng, dims, pieces, smallest, largest):
    factor_of = 1.0
    for axis_at, parts in pieces:
        heights = jax.random.uniform(jax.random.fold_in(jax.random.fold_in(rng, 6), axis_at), (parts,), jnp.float32, smallest / len(pieces), largest / len(pieces))
        factor_of = factor_of * jnp.repeat(jnp.exp(heights), dims[axis_at] // parts).reshape((-1,) + (1,) * (len(dims) - 1 - axis_at))
    return factor_of


def centred(rng, shape, width, bound, pieces=(), kind=jnp.bfloat16):
    gain = levels(rng, shape, pieces, -0.22, 0.18) if pieces else 1.0
    values = jax.random.normal(rng, shape, jnp.float32) * width * gain
    return jnp.minimum(jnp.maximum(values, -bound), bound).astype(kind)


def setup_inputs(seed: int = 0) -> dict:
    splits = jax.random.split(jax.random.key(seed), 11)
    adj_init = centred(splits[0], (NV, NX, NW, NS), 0.2, 1.2, ((1, 4), (2, 16), (3, 8)), jnp.float32)
    adj_source = centred(splits[1], (NV, NX, NW, NS), 2.0, 12.0, ((1, 4), (2, 16), (3, 8)), jnp.float32)
    velocity = centred(splits[2], (3, NX, NW, NS), 1.0, 4.0, ((1, 4), (2, 16), (3, 8)), jnp.float32)
    sound = jnp.clip(jnp.exp(math.log(2.0) - 1.3862944 * jax.random.uniform(splits[3], (NX, NW, NS), jnp.float32) ** levels(splits[3], (NX, NW, NS), ((0, 4), (1, 16), (2, 8)), -0.2, 0.2)), 0.5, 2.0)
    face_couple = centred(splits[4], (3, 2, NV, NV), 0.06, 0.36, (), jnp.float32)
    precond_inv = draw_precond_inv(jax.random.fold_in(splits[10], 71), 0)
    wall_code = touch_ends(jax.random.randint(splits[6], (NX, NS), 0, 4), jax.random.fold_in(splits[6], 1), 0, 3).astype(jnp.int32)
    spall_mask = touch_ends((jax.random.randint(splits[7], (NX, NS), 0, 4) < 1).astype(jnp.int32), jax.random.fold_in(splits[7], 1), 0, 1)
    wall_table = jnp.clip(jnp.exp(jax.random.uniform(splits[8], (KINDS, NV), jnp.float32, math.log(0.5), math.log(2.0))), 0.5, 2.0)
    spall_gain = jnp.clip(jnp.exp(jax.random.uniform(splits[9], (NV,), jnp.float32, math.log(0.5), math.log(3.0))), 0.5, 3.0)
    return dict(adj_init=adj_init, adj_source=adj_source, velocity=velocity, sound=sound, face_couple=face_couple, precond_inv=precond_inv, wall_code=wall_code, spall_mask=spall_mask, wall_table=wall_table, spall_gain=spall_gain)


def shifted(field, direction, facing):
    if direction == 2:
        return jnp.roll(field, 1 if facing == 0 else -1, axis=3)
    widths = [(0, 0), (0, 0), (0, 0), (0, 0)]
    widths[direction + 1] = (1, 1)
    padded = jnp.pad(field, widths)
    if direction == 0:
        return padded[:, :-2] if facing == 0 else padded[:, 2:]
    return padded[:, :, :-2] if facing == 0 else padded[:, :, 2:]


def make_wall_coef(wall_code, spall_mask, wall_table, spall_gain):
    kinds_ids = jnp.arange(wall_table.shape[0], dtype=jnp.int32)
    onehot = (wall_code[None] == kinds_ids[:, None, None]).astype(jnp.float32)
    table_part = jnp.einsum('ki,krc->irc', wall_table, onehot, precision=lax.Precision.HIGHEST)
    return table_part + spall_gain[:, None, None] * spall_mask.astype(jnp.float32)[None]


def reference(adj_init, adj_source, velocity, sound, face_couple, precond_inv, wall_code, spall_mask, wall_table, spall_gain):
    radius = jnp.abs(velocity) + sound[None]
    wall_coef = make_wall_coef(wall_code, spall_mask, wall_table, spall_gain)
    adjoint = adj_init
    residual = adj_source
    for sweep_index in range(SWEEPS):
        rate_sum = jnp.ones_like(radius[0])
        flow_sum = jnp.zeros_like(adjoint)
        for direction in range(3):
            for facing in range(2):
                face_rate = 0.5 * (radius[direction] + shifted(radius, direction, facing)[direction])
                coupled = jnp.einsum('ji,jxyz->ixyz', face_couple[direction, facing], shifted(adjoint, direction, facing), precision=lax.Precision.HIGHEST)
                flow_sum = flow_sum + face_rate[None] * coupled
                rate_sum = rate_sum + face_rate
        residual = adj_source - rate_sum[None] * adjoint - flow_sum
        wall_term = radius[1][:, 0, :][None] * wall_coef * adjoint[:, :, 0, :]
        residual = residual.at[:, :, 0, :].add(-wall_term)
        update = jnp.einsum('ij,jxyz->ixyz', precond_inv, residual, precision=lax.Precision.HIGHEST)
        adjoint = adjoint + update / rate_sum[None]
    return adjoint, residual
```

```python
import jax
import jax.numpy as jnp
from jax import lax
from jax.experimental import pallas as pl
from jax.experimental.pallas import tpu as pltpu
from jax.sharding import PartitionSpec as P

NV = 17
X = 12
WL = 8
L = 128
B1 = 144
ROWS = NV * WL
PAIRS = X // 2
R1, R0, R2 = 17, 18, 19
WROWS = 18 * X
F32, BF = jnp.float32, jnp.bfloat16
HI = lax.Precision.HIGHEST
MESH = pl.DeviceIdType.MESH


def iota(shape, dim):
    return lax.broadcasted_iota(jnp.int32, shape, dim)


def dot(a, b):
    return lax.dot_general(a, b, (((1,), (0,)), ((), ())), preferred_element_type=F32)


def dot_nt(a, b):
    return lax.dot_general(a, b, (((1,), (1,)), ((), ())), preferred_element_type=F32)


def split(v):
    hi = v.astype(BF)
    return hi, (v - hi.astype(F32)).astype(BF)


def stacked(hi, lo, rows):
    parts = [hi, lo, hi]
    short = rows - 3 * hi.shape[0]
    return jnp.concatenate(parts + [jnp.zeros((short, hi.shape[1]), BF)], axis=0)


def hi_lo(weights, from_lo):
    hi = weights.astype(BF).astype(F32)
    return jnp.where(from_lo, weights - hi, hi).astype(BF)


def build_weights(fc, pinv, w_all, w_p, w_span, w_wall):
    spread = (iota((B1, NV), 0) // WL == iota((B1, NV), 1)).astype(F32)

    def rows_of(couple):
        return lax.dot_general(spread, couple, (((1,), (1,)), ((), ())), precision=HI, preferred_element_type=F32)

    k = iota((B1, 512), 1)
    kk = jnp.where(k >= 2 * B1, k - 2 * B1, jnp.where(k >= B1, k - B1, k))
    used = k < 3 * B1
    kj = iota((2 * NV, 512), 1)
    kj = jnp.where(kj >= 2 * B1, kj - 2 * B1, jnp.where(kj >= B1, kj - B1, kj))
    js = iota((2 * NV, 512), 0)
    lanes = [((kj // WL == js // 2) & (js % 2 == s)).astype(F32) for s in range(2)]
    p_lanes = (kj[:NV] // WL == js[:NV]).astype(F32)
    w = iota((B1, 512), 0) % WL
    wk = kk % WL

    def expand(rows, lanes, shift):
        full = lax.dot_general(rows, lanes, (((1,), (0,)), ((), ())), precision=HI, preferred_element_type=F32)
        full = jnp.where(used & (wk == w + shift), full, 0.0)
        hi = full.astype(BF).astype(F32)
        return jnp.where(k >= 2 * B1, full - hi, hi)

    rows = [rows_of(fc[d].reshape(2 * NV, NV)) for d in range(3)]
    for d in range(3):
        shifts = (-1, 1) if d == 1 else (0, 0)
        both = [expand(rows[d], lanes[s], shifts[s])[:ROWS] for s in range(2)]
        w_all[2 * ROWS * d : 2 * ROWS * (d + 1), :] = jnp.concatenate(both, axis=0).astype(BF)
    p_rows = lax.dot_general(spread, pinv[...], (((1,), (0,)), ((), ())), precision=HI, preferred_element_type=F32)
    w_p[...] = expand(p_rows, p_lanes, 0).astype(BF)

    ks = iota((B1, 256), 1)
    rs = iota((B1, 256), 0)
    js = iota((2 * NV, 256), 0)
    kj = iota((2 * NV, 256), 1)
    for s in range(2):
        s_lanes = ((kj // WL == js // 2) & (js % 2 == s)).astype(F32)
        full = lax.dot_general(rows[2], s_lanes, (((1,), (0,)), ((), ())), precision=HI, preferred_element_type=F32)
        full = jnp.where((rs % WL == ks % WL) & (ks < ROWS), full, 0.0)
        full = jnp.where((rs >= ROWS) & (rs == ks), 1.0, full)
        hi = full.astype(BF)
        lo = (full - hi.astype(F32)).astype(BF)
        w_span[:, 768 * s : 768 * s + 256] = hi
        w_span[:, 768 * s + 256 : 768 * s + 512] = hi
        w_span[:, 768 * s + 512 : 768 * s + 768] = lo

    def mod48(v):
        return jnp.where(v >= 96, v - 96, jnp.where(v >= 48, v - 48, v))

    kw = mod48(ks)
    kv = mod48(kj)
    full = 0.0
    for s in range(2):
        pick = ((kv - 24 * s == js // 2) & (js % 2 == s)).astype(F32)
        part = lax.dot_general(rows[1], pick, (((1,), (0,)), ((), ())), precision=HI, preferred_element_type=F32)
        full = full + jnp.where(rs % WL == (WL - 1) * s, part, 0.0)
    full = jnp.where((ks < 144) & (rs < ROWS), full, 0.0)
    w_wall[...] = hi_lo(full, ks >= 96)


def kernel(
    adj_in, src_in, vel_in, snd_in, code_in, mask_in, fc_in, pinv_in, table_in, gain_in,
    adj_out, res_out,
    ar, src, vel, snd, code, mask, fc, pinv, table, gain, res, split_a, g_buf, diag,
    w_all, w_p, w_span, w_wall, take, tg,
    send_s, send_w, send_p, recv_s, recv_w, recv_p, spread, rates,
    in_sem, send_sem, recv_sem,
):
    st, sp, wl = (lax.axis_index(a) for a in ("stream", "span", "wall"))
    n_st, n_sp, n_wl = (lax.axis_size(a) for a in ("stream", "span", "wall"))
    right, left = lax.rem(sp + 1, n_sp), lax.rem(sp + n_sp - 1, n_sp)
    ways = [
        ({"stream": st + 1}, st < n_st - 1, st > 0),
        ({"stream": st - 1}, st > 0, st < n_st - 1),
        ({"wall": wl + 1}, wl < n_wl - 1, wl > 0),
        ({"wall": wl - 1}, wl > 0, wl < n_wl - 1),
        ({"span": right}, None, None),
        ({"span": left}, None, None),
    ]

    def when(cond, fn):
        if cond is None:
            fn()
        else:
            pl.when(cond)(fn)

    barrier = pltpu.get_barrier_semaphore()
    for device, sends, _ in ways:
        when(sends, lambda device=device: pl.semaphore_signal(barrier, inc=1, device_id=device, device_id_type=MESH))

    loads = [
        pltpu.make_async_copy(adj_in, ar.at[0 : NV * X * WL, :], in_sem.at[0]),
        pltpu.make_async_copy(vel_in, vel, in_sem.at[1]),
        pltpu.make_async_copy(snd_in, snd, in_sem.at[2]),
        pltpu.make_async_copy(src_in, src, in_sem.at[3]),
    ]
    small = [
        pltpu.make_async_copy(fc_in, fc, in_sem.at[6]),
        pltpu.make_async_copy(pinv_in, pinv, in_sem.at[7]),
        pltpu.make_async_copy(table_in, table, in_sem.at[8]),
        pltpu.make_async_copy(gain_in, gain, in_sem.at[9]),
    ]
    for c in small + loads:
        c.start()
    row0 = pl.multiple_of(X * st - 4 * lax.rem(st, 2), 8)
    off = 4 * lax.rem(st, 2)
    col0 = pl.multiple_of(L * sp, L)
    at_wall = wl == 0
    code_loads = [
        pltpu.make_async_copy(code_in.at[pl.ds(row0, 16), pl.ds(col0, L)], code, in_sem.at[4]),
        pltpu.make_async_copy(mask_in.at[pl.ds(row0, 16), pl.ds(col0, L)], mask, in_sem.at[5]),
    ]

    @pl.when(at_wall)
    def _():
        for c in code_loads:
            c.start()

    for r in range(2):
        for side in range(2):
            recv_w[r, side, WROWS:, :] = jnp.zeros((recv_w.shape[2] - WROWS, L), F32)
            spread[side] = jnp.zeros((2, 32, L), F32)
            send_p[r, side] = jnp.zeros((2, 16, L), F32)

            @pl.when(jnp.logical_not(ways[side][2]))
            def _():
                recv_s[r, side] = jnp.zeros((18, WL, L), F32)

            @pl.when(jnp.logical_not(ways[2 + side][2]))
            def _():
                recv_w[r, side, 0:WROWS, :] = jnp.zeros((WROWS, L), F32)

    g_buf[0, 0:ROWS, :] = jnp.zeros((ROWS, 2 * L), F32)
    g_buf[PAIRS + 1, ROWS : 2 * ROWS, :] = jnp.zeros((ROWS, 2 * L), F32)
    t_row, t_col = iota((32, 256 * X), 0), iota((32, 256 * X), 1)
    take_at = jnp.where(t_row < 16, L - 1, 0) + L * lax.rem(t_col // L, 2)
    take[...] = ((t_col // 256 == t_row % 16) & (t_col % 256 == take_at)).astype(BF)
    for c in small:
        c.wait()
    build_weights(fc, pinv, w_all, w_p, w_span, w_wall)

    for c in loads[:3]:
        c.wait()
    for d, slot in ((0, R0), (1, R1), (2, R2)):
        ar[slot * X * WL : (slot + 1) * X * WL, :] = (jnp.abs(vel[d]) + snd[...]).reshape(X * WL, L)

    def at(slot, x):
        start = slot * X * WL + x * WL
        return pl.ds(start if isinstance(start, int) else pl.multiple_of(start, WL), WL)

    def one(slot, x):
        return ar[at(slot, x), :]

    def plane(x):
        return jnp.concatenate([one(j, x) for j in range(NV)], axis=0)

    def plane3(x):
        return plane(x).reshape(NV, WL, L)

    def store_split(x, value):
        hi, lo = split(jnp.concatenate([value, one(R2, x)], axis=0))
        split_a[x, 0] = hi
        split_a[x, 1] = lo

    def first_split(x, _):
        store_split(x, plane(x))
        return 0

    lax.fori_loop(0, X, first_split, 0)

    def copies(r):
        out = []
        for n, (device, _, _) in enumerate(ways):
            bufs = ((send_s, recv_s), (send_w, recv_w), (send_p, recv_p))[n // 2]
            side = n % 2
            if n // 2 == 1:
                dst = bufs[1].at[r, side, 0:WROWS, :]
            else:
                dst = bufs[1].at[r, side]
            out.append(
                pltpu.make_async_remote_copy(
                    src_ref=bufs[0].at[r, side],
                    dst_ref=dst,
                    send_sem=send_sem.at[r, n],
                    recv_sem=recv_sem.at[r, n],
                    device_id=device,
                    device_id_type=MESH,
                )
            )
        return out

    def pack(r):
        faces = jnp.concatenate([split_a[x, h] for x in range(X) for h in range(2)], axis=1)
        both = dot_nt(take[...], faces)
        for side in range(2):
            send_p[r, side, 0] = both[16 * side : 16 * side + 16, 0:L]
            send_p[r, side, 1, :, 0 : B1 - L] = both[16 * side : 16 * side + 16, L:B1]
        for side, w in ((0, WL - 1), (1, 0)):
            send_w[r, side] = ar[pl.ds(w, WROWS, stride=WL), :]
        for side, x in ((0, X - 1), (1, 0)):
            send_s[r, side, 0:NV] = plane3(x)
            send_s[r, side, NV] = one(R0, x)

    def send(r):
        for n, c in enumerate(copies(r)):
            when(ways[n][1], c.start)

    def receive(r):
        for n, c in enumerate(copies(r)):
            when(ways[n][2], c.wait_recv)

    lane = iota((WL, L), 1)
    sub = iota((WL, L), 0)

    def planes_rhs(hi_lo_pairs):
        return jnp.concatenate([stacked(h, l, 512) for h, l in hi_lo_pairs], axis=1)

    def local():
        def couple(p, _):
            rhs = planes_rhs([(split_a[2 * p + q, 0], split_a[2 * p + q, 1]) for q in range(2)])
            g_buf[p + 1] = dot(w_all[...], rhs)
            return 0

        lax.fori_loop(0, PAIRS, couple, 0)

        def gather(p, _):
            for q in range(2):
                x = 2 * p + q
                here = slice(q * L, (q + 1) * L)
                r0, r1, r2 = one(R0, x), one(R1, x), one(R2, x)
                m00 = 0.5 * (r0 + one(R0, jnp.maximum(x - 1, 0)))
                m01 = 0.5 * (r0 + one(R0, jnp.minimum(x + 1, X - 1)))
                m10 = 0.5 * (r1 + pltpu.roll(r1, 1, 0))
                m11 = 0.5 * (r1 + pltpu.roll(r1, WL - 1, 0))
                m20 = jnp.where(lane == 0, 0.0, 0.5 * (r2 + pltpu.roll(r2, 1, 1)))
                m21 = jnp.where(lane == L - 1, 0.0, 0.5 * (r2 + pltpu.roll(r2, L - 1, 1)))

                def g(page, n, part):
                    return g_buf[page, n * ROWS : (n + 1) * ROWS, part]

                lower, upper = slice(0, L), slice(L, 2 * L)
                g00 = g(p + 1, 0, lower) if q == 1 else g(p, 0, upper)
                g01 = g(p + 2, 1, lower) if q == 1 else g(p + 1, 1, upper)
                terms = [
                    (m00, g00),
                    (m01, g01),
                    (m10, g(p + 1, 2, here)),
                    (m11, g(p + 1, 3, here)),
                    (m20, pltpu.roll(g(p + 1, 4, here), 1, 1)),
                    (m21, pltpu.roll(g(p + 1, 5, here), L - 1, 1)),
                ]
                total = src[:, x]
                for m, v in terms:
                    total = total - m[None] * v.reshape(NV, WL, L)
                res[:, x] = total
            return 0

        lax.fori_loop(0, PAIRS, gather, 0)

        @pl.when(at_wall)
        def _():
            def wall_term(x, _):
                res[:, x] = res[:, x] - diag[:, x] * plane3(x)
                return 0

            lax.fori_loop(0, X, wall_term, 0)

    def finish(r, last):
        for side in range(2):
            for half in range(2):
                spread[side, half, pl.ds(2 - side, X, stride=2), :] = recv_p[r, side, half, 0:X, :]
        cols = []
        for side in range(2):
            hi, lo = split(jnp.concatenate([spread[side, 0], spread[side, 1]], axis=1))
            cols += [hi, lo, hi]
        cols = jnp.concatenate(cols, axis=1)
        cols = jnp.concatenate([cols, jnp.zeros((L - 32, cols.shape[1]), BF)], axis=0)
        edge_cols = dot_nt(w_span[...], cols)

        ends = [split(recv_s[r, side].reshape(B1, L)) for side in range(2)]
        g_ends = dot(w_all[0 : 2 * ROWS, :], planes_rhs(ends))
        for side, x in ((0, 0), (1, X - 1)):
            rate = 0.5 * (one(R0, x) + recv_s[r, side, NV])
            g_end = g_ends[side * ROWS : (side + 1) * ROWS, side * L : (side + 1) * L]
            res[:, x] = res[:, x] - rate[None] * g_end.reshape(NV, WL, L)

        for p in range(PAIRS):
            xs = (2 * p, 2 * p + 1)
            rhs = []
            for x in xs:
                rows = jnp.concatenate([recv_w[r, side, pl.ds(x, 24, stride=X), :] for side in range(2)], axis=0)
                rhs.append(stacked(*split(rows), 256))
            g_wall = dot(w_wall[...], jnp.concatenate(rhs, axis=1))
            parts = []
            for q, x in enumerate(xs):
                edge = pltpu.roll(edge_cols, (2 * L - 2 * x - 2) % L, 1)
                if r == 0:
                    r0, r1, r2 = one(R0, x), one(R1, x), one(R2, x)
                    r0m = recv_s[r, 0, NV] if x == 0 else one(R0, x - 1)
                    r0p = recv_s[r, 1, NV] if x == X - 1 else one(R0, x + 1)
                    low = recv_w[r, 0, NV * X + x : NV * X + x + 1, :]
                    high = recv_w[r, 1, NV * X + x : NV * X + x + 1, :]
                    r1m = jnp.where(sub == 0, jnp.broadcast_to(low, (WL, L)), pltpu.roll(r1, 1, 0))
                    r1p = jnp.where(sub == WL - 1, jnp.broadcast_to(high, (WL, L)), pltpu.roll(r1, WL - 1, 0))
                    beyond = edge[ROWS:B1]
                    r2m = jnp.where(lane == 0, beyond, pltpu.roll(r2, 1, 1))
                    r2p = jnp.where(lane == L - 1, beyond, pltpu.roll(r2, L - 1, 1))
                    total = 1.0 + (r0 + r1 + r2) + 0.5 * ((r0m + r0p) + (r1m + r1p) + (r2m + r2p))
                    rate_w = jnp.where(sub == 0, 0.5 * (r1 + r1m), jnp.where(sub == WL - 1, 0.5 * (r1 + r1p), 0.0))
                    rate_s = jnp.where(lane == 0, 0.5 * (r2 + r2m), jnp.where(lane == L - 1, 0.5 * (r2 + r2p), 0.0))
                    rates[x, 0] = total
                    rates[x, 1] = 1.0 / total
                    rates[x, 2] = rate_w
                    rates[x, 3] = rate_s
                total, rate_w, rate_s = rates[x, 0], rates[x, 2], rates[x, 3]
                value = res[:, x] - total[None] * plane3(x)
                value = value - rate_w[None] * g_wall[0:ROWS, q * L : (q + 1) * L].reshape(NV, WL, L)
                value = value - rate_s[None] * edge[0:ROWS].reshape(NV, WL, L)
                if last:
                    res_out[:, x] = value
                value = jnp.concatenate([value.reshape(ROWS, L), jnp.zeros((WL, L), F32)], axis=0)
                parts.append(split(value))
            update = dot(w_p[...], planes_rhs(parts))
            for q, x in enumerate(xs):
                step = update[0:ROWS, q * L : (q + 1) * L].reshape(NV, WL, L)
                value = plane3(x) + step * rates[x, 1][None]
                if last:
                    adj_out[:, x] = value
                else:
                    for j in range(NV):
                        ar[at(j, x), :] = value[j]
                    store_split(x, value.reshape(ROWS, L))

    pack(0)
    pl.semaphore_wait(
        barrier,
        2
        + (st > 0).astype(jnp.int32)
        + (st < n_st - 1).astype(jnp.int32)
        + (wl > 0).astype(jnp.int32)
        + (wl < n_wl - 1).astype(jnp.int32),
    )
    send(0)

    @pl.when(at_wall)
    def _():
        for c in code_loads:
            c.wait()
        tg[...] = jnp.zeros((8, NV), F32)
        tg[0:4, :] = table[...]
        tg[4:5, :] = gain[...]
        own = (iota((ROWS, NV), 0) == WL * iota((ROWS, NV), 1)).astype(F32)
        coef = lax.dot_general(own, tg[...], (((1,), (1,)), ((), ())), precision=HI, preferred_element_type=F32)

        def coef_of(x, _):
            codes = jnp.broadcast_to(code[pl.ds(x + off, 1), :], (8, L))
            spall = jnp.broadcast_to(mask[pl.ds(x + off, 1), :], (8, L))
            hot = jnp.where(sub < 4, (codes == sub).astype(F32), jnp.where(sub == 4, spall.astype(F32), 0.0))
            wall = lax.dot_general(coef, hot, (((1,), (0,)), ((), ())), precision=HI, preferred_element_type=F32)
            diag[:, x] = one(R1, x)[None] * wall.reshape(NV, WL, L)
            return 0

        lax.fori_loop(0, X, coef_of, 0)

    loads[3].wait()
    local()
    receive(0)
    finish(0, False)
    pack(1)
    send(1)
    local()
    receive(1)
    finish(1, True)
    for r in range(2):
        for n, c in enumerate(copies(r)):
            when(ways[n][1], c.wait_send)


def on_device(adj_init, adj_source, velocity, sound, face_couple, precond_inv, wall_code, spall_mask, wall_table, spall_gain):
    field = jax.ShapeDtypeStruct((NV, X, WL, L), F32)
    hbm = pl.BlockSpec(memory_space=pltpu.HBM)
    inside = pl.BlockSpec(memory_space=pltpu.VMEM)
    return pl.pallas_call(
        kernel,
        out_shape=(field, field),
        in_specs=[hbm] * 10,
        out_specs=(inside, inside),
        scratch_shapes=[
            pltpu.VMEM((20 * X * WL, L), F32),
            pltpu.VMEM((NV, X, WL, L), F32),
            pltpu.VMEM((3, X, WL, L), F32),
            pltpu.VMEM((X, WL, L), F32),
            pltpu.VMEM((16, L), jnp.int32),
            pltpu.VMEM((16, L), jnp.int32),
            pltpu.VMEM((3, NV, 2, NV), F32),
            pltpu.VMEM((NV, NV), F32),
            pltpu.VMEM((4, NV), F32),
            pltpu.VMEM((1, NV), F32),
            pltpu.VMEM((NV, X, WL, L), F32),
            pltpu.VMEM((X, 2, B1, L), BF),
            pltpu.VMEM((PAIRS + 2, 6 * ROWS, 2 * L), F32),
            pltpu.VMEM((NV, X, WL, L), F32),
            pltpu.VMEM((6 * ROWS, 512), BF),
            pltpu.VMEM((B1, 512), BF),
            pltpu.VMEM((B1, 1536), BF),
            pltpu.VMEM((B1, 256), BF),
            pltpu.VMEM((32, 256 * X), BF),
            pltpu.VMEM((8, NV), F32),
            pltpu.VMEM((2, 2, 18, WL, L), F32),
            pltpu.VMEM((2, 2, WROWS, L), F32),
            pltpu.VMEM((2, 2, 2, 16, L), F32),
            pltpu.VMEM((2, 2, 18, WL, L), F32),
            pltpu.VMEM((2, 2, 24 * X, L), F32),
            pltpu.VMEM((2, 2, 2, 16, L), F32),
            pltpu.VMEM((2, 2, 32, L), F32),
            pltpu.VMEM((X, 4, WL, L), F32),
            pltpu.SemaphoreType.DMA((10,)),
            pltpu.SemaphoreType.DMA((2, 6)),
            pltpu.SemaphoreType.DMA((2, 6)),
        ],
        compiler_params=pltpu.CompilerParams(collective_id=0, has_side_effects=True, vmem_limit_bytes=67000000),
        name="sweeps",
    )(
        adj_init.reshape(NV * X * WL, L),
        adj_source,
        velocity,
        sound,
        wall_code,
        spall_mask,
        face_couple.transpose(0, 2, 1, 3),
        precond_inv,
        wall_table,
        spall_gain.reshape(1, NV),
    )


def solution(mesh):
    field = P(None, "stream", "wall", "span")
    return jax.shard_map(
        on_device,
        mesh=mesh,
        in_specs=(field, field, field, P("stream", "wall", "span"), P(), P(), P(), P(), P(), P()),
        out_specs=(field, field),
        check_vma=False,
    )
```

```python
import jax
import jax.numpy as jnp
from jax import lax
from jax.experimental import pallas as pl
from jax.experimental.pallas import tpu as pltpu
from jax.sharding import PartitionSpec as P

NV = 17
X = 12
WL = 8
L = 128
B1 = 144
ROWS = NV * WL
PAIRS = X // 2
R1, R0, R2 = 17, 18, 19
WROWS = 18 * X
F32, BF = jnp.float32, jnp.bfloat16
HI = lax.Precision.HIGHEST
MESH = pl.DeviceIdType.MESH


def iota(shape, dim):
    return lax.broadcasted_iota(jnp.int32, shape, dim)


def dot(a, b):
    return lax.dot_general(a, b, (((1,), (0,)), ((), ())), preferred_element_type=F32)


def dot_nt(a, b):
    return lax.dot_general(a, b, (((1,), (1,)), ((), ())), preferred_element_type=F32)


def split(v):
    hi = v.astype(BF)
    return hi, (v - hi.astype(F32)).astype(BF)


def stacked(hi, lo, rows):
    parts = [hi, lo, hi]
    short = rows - 3 * hi.shape[0]
    return jnp.concatenate(parts + [jnp.zeros((short, hi.shape[1]), BF)], axis=0)


def build_weights(fc, pinv, w_all, w_p, w_span, w_wall):
    spread = (iota((B1, NV), 0) // WL == iota((B1, NV), 1)).astype(BF)
    both = [jnp.concatenate(split(fc[d].reshape(2 * NV, NV)), axis=0) for d in range(3)]
    rows = [dot_nt(spread, v).astype(BF) for v in both]
    p_rows = jnp.concatenate([dot(spread, v).astype(BF) for v in split(pinv[...])], axis=1)

    def fold(k, length):
        return jnp.where(k >= 2 * length, k - 2 * length, jnp.where(k >= length, k - length, k))

    def picker(n_rows, width, length, s, low_at):
        js, k = iota((2 * n_rows, width), 0), iota((2 * n_rows, width), 1)
        low = js >= n_rows
        js = jnp.where(low, js - n_rows, js)
        kk = fold(k, length) if length else k
        if s is None:
            return js, k, kk, low == (k >= low_at)
        return js // 2, k, kk, (low == (k >= low_at)) & (js % 2 == s)

    k = iota((B1, 512), 1)
    w = iota((B1, 512), 0) % WL
    wk = fold(k, B1) % WL

    def expand(values, pick, shift):
        return jnp.where(wk == w + shift, dot(values, pick), 0.0)

    picks = []
    for s in range(2):
        j, kc, kk, ok = picker(2 * NV, 512, B1, s, 2 * B1)
        picks.append((ok & (kk // WL == j) & (kc < 3 * B1)).astype(BF))
    for d in range(3):
        shifts = (-1, 1) if d == 1 else (0, 0)
        pair = [expand(rows[d], picks[s], shifts[s])[:ROWS] for s in range(2)]
        w_all[2 * ROWS * d : 2 * ROWS * (d + 1), :] = jnp.concatenate(pair, axis=0).astype(BF)
    j, kc, kk, ok = picker(NV, 512, B1, None, 2 * B1)
    p_pick = (ok & (kk // WL == j) & (kc < 3 * B1)).astype(BF)
    w_p[...] = expand(p_rows, p_pick, 0).astype(BF)

    ks = iota((B1, 512), 1)
    rs = iota((B1, 512), 0)
    low_half = ks >= 256
    kq = jnp.where(low_half, ks - 256, ks)
    for s in range(2):
        j, kc, kk, ok = picker(2 * NV, 512, 0, s, 256)
        kk = jnp.where(kc >= 256, kc - 256, kc)
        full = dot(rows[2], (ok & (kk // WL == j)).astype(BF))
        full = jnp.where((rs % WL == kq % WL) & (kq < ROWS), full, 0.0)
        full = jnp.where((rs >= ROWS) & (rs == ks), 1.0, full).astype(BF)
        w_span[:, 768 * s : 768 * s + 256] = full[:, 0:256]
        w_span[:, 768 * s + 256 : 768 * s + 768] = full

    ks, rs = iota((B1, 256), 1), iota((B1, 256), 0)
    full = 0.0
    for s in range(2):
        j, kc, kk, ok = picker(2 * NV, 256, 48, s, 96)
        part = dot(rows[1], (ok & (kk - 24 * s == j) & (kc < 144)).astype(BF))
        full = full + jnp.where(rs % WL == (WL - 1) * s, part, 0.0)
    w_wall[...] = jnp.where(rs < ROWS, full, 0.0).astype(BF)


def kernel(
    adj_in, src_in, vel_in, snd_in, code_in, mask_in, fc_in, pinv_in, table_in, gain_in,
    adj_out, res_out,
    ar, src, vel, snd, code, mask, fc, pinv, table, gain, res, split_a, g_buf, diag,
    w_all, w_p, w_span, w_wall, take, tg,
    send_s, send_w, send_p, recv_s, recv_w, recv_p, spread, rates,
    in_sem, send_sem, recv_sem,
):
    st, sp, wl = (lax.axis_index(a) for a in ("stream", "span", "wall"))
    n_st, n_sp, n_wl = (lax.axis_size(a) for a in ("stream", "span", "wall"))
    right, left = lax.rem(sp + 1, n_sp), lax.rem(sp + n_sp - 1, n_sp)
    ways = [
        ({"stream": st + 1}, st < n_st - 1, st > 0),
        ({"stream": st - 1}, st > 0, st < n_st - 1),
        ({"wall": wl + 1}, wl < n_wl - 1, wl > 0),
        ({"wall": wl - 1}, wl > 0, wl < n_wl - 1),
        ({"span": right}, None, None),
        ({"span": left}, None, None),
    ]

    def when(cond, fn):
        if cond is None:
            fn()
        else:
            pl.when(cond)(fn)

    barrier = pltpu.get_barrier_semaphore()
    for device, sends, _ in ways:
        when(sends, lambda device=device: pl.semaphore_signal(barrier, inc=1, device_id=device, device_id_type=MESH))

    loads = [
        pltpu.make_async_copy(adj_in, ar.at[0 : NV * X * WL, :], in_sem.at[0]),
        pltpu.make_async_copy(vel_in, vel, in_sem.at[1]),
        pltpu.make_async_copy(snd_in, snd, in_sem.at[2]),
        pltpu.make_async_copy(src_in, src, in_sem.at[3]),
    ]
    small = [
        pltpu.make_async_copy(fc_in, fc, in_sem.at[6]),
        pltpu.make_async_copy(pinv_in, pinv, in_sem.at[7]),
        pltpu.make_async_copy(table_in, table, in_sem.at[8]),
        pltpu.make_async_copy(gain_in, gain, in_sem.at[9]),
    ]
    for c in small + loads:
        c.start()
    row0 = pl.multiple_of(X * st - 4 * lax.rem(st, 2), 8)
    off = 4 * lax.rem(st, 2)
    col0 = pl.multiple_of(L * sp, L)
    at_wall = wl == 0
    code_loads = [
        pltpu.make_async_copy(code_in.at[pl.ds(row0, 16), pl.ds(col0, L)], code, in_sem.at[4]),
        pltpu.make_async_copy(mask_in.at[pl.ds(row0, 16), pl.ds(col0, L)], mask, in_sem.at[5]),
    ]

    @pl.when(at_wall)
    def _():
        for c in code_loads:
            c.start()

    for r in range(2):
        for side in range(2):
            recv_w[r, side, WROWS:, :] = jnp.zeros((recv_w.shape[2] - WROWS, L), F32)
            spread[side] = jnp.zeros((2, 32, L), F32)
            send_p[r, side] = jnp.zeros((2, 16, L), F32)

            @pl.when(jnp.logical_not(ways[side][2]))
            def _():
                recv_s[r, side] = jnp.zeros((18, WL, L), F32)

            @pl.when(jnp.logical_not(ways[2 + side][2]))
            def _():
                recv_w[r, side, 0:WROWS, :] = jnp.zeros((WROWS, L), F32)

    g_buf[0, 0:ROWS, :] = jnp.zeros((ROWS, 2 * L), F32)
    g_buf[PAIRS + 1, ROWS : 2 * ROWS, :] = jnp.zeros((ROWS, 2 * L), F32)
    t_row, t_col = iota((32, 256 * X), 0), iota((32, 256 * X), 1)
    take_at = jnp.where(t_row < 16, L - 1, 0) + L * lax.rem(t_col // L, 2)
    take[...] = ((t_col // 256 == t_row % 16) & (t_col % 256 == take_at)).astype(BF)
    for c in loads[:3]:
        c.wait()
    for d, slot in ((0, R0), (1, R1), (2, R2)):
        ar[slot * X * WL : (slot + 1) * X * WL, :] = (jnp.abs(vel[d]) + snd[...]).reshape(X * WL, L)

    def at(slot, x):
        start = slot * X * WL + x * WL
        return pl.ds(start if isinstance(start, int) else pl.multiple_of(start, WL), WL)

    def one(slot, x):
        return ar[at(slot, x), :]

    def plane(x):
        return jnp.concatenate([one(j, x) for j in range(NV)], axis=0)

    def plane3(x):
        return plane(x).reshape(NV, WL, L)

    def store_split(x, value):
        hi, lo = split(jnp.concatenate([value, one(R2, x)], axis=0))
        split_a[x, 0] = hi
        split_a[x, 1] = lo

    def first_split(x, _):
        store_split(x, plane(x))
        return 0

    lax.fori_loop(0, X, first_split, 0)

    def copies(r):
        out = []
        for n, (device, _, _) in enumerate(ways):
            bufs = ((send_s, recv_s), (send_w, recv_w), (send_p, recv_p))[n // 2]
            side = n % 2
            if n // 2 == 1:
                dst = bufs[1].at[r, side, 0:WROWS, :]
            else:
                dst = bufs[1].at[r, side]
            out.append(
                pltpu.make_async_remote_copy(
                    src_ref=bufs[0].at[r, side],
                    dst_ref=dst,
                    send_sem=send_sem.at[r, n],
                    recv_sem=recv_sem.at[r, n],
                    device_id=device,
                    device_id_type=MESH,
                )
            )
        return out

    def pack(r):
        faces = jnp.concatenate([split_a[x, h] for x in range(X) for h in range(2)], axis=1)
        both = dot_nt(take[...], faces)
        for side in range(2):
            send_p[r, side, 0] = both[16 * side : 16 * side + 16, 0:L]
            send_p[r, side, 1, :, 0 : B1 - L] = both[16 * side : 16 * side + 16, L:B1]
        for side, w in ((0, WL - 1), (1, 0)):
            send_w[r, side] = ar[pl.ds(w, WROWS, stride=WL), :]
        for side, x in ((0, X - 1), (1, 0)):
            send_s[r, side, 0:NV] = plane3(x)
            send_s[r, side, NV] = one(R0, x)

    def send(r):
        for n, c in enumerate(copies(r)):
            when(ways[n][1], c.start)

    def receive(r):
        for n, c in enumerate(copies(r)):
            when(ways[n][2], c.wait_recv)

    lane = iota((WL, L), 1)
    sub = iota((WL, L), 0)

    def planes_rhs(hi_lo_pairs):
        return jnp.concatenate([stacked(h, l, 512) for h, l in hi_lo_pairs], axis=1)

    def local():
        def couple(p, _):
            rhs = planes_rhs([(split_a[2 * p + q, 0], split_a[2 * p + q, 1]) for q in range(2)])
            g_buf[p + 1] = dot(w_all[...], rhs)
            return 0

        lax.fori_loop(0, PAIRS, couple, 0)

        def gather(p, _):
            for q in range(2):
                x = 2 * p + q
                here = slice(q * L, (q + 1) * L)
                r0, r1, r2 = one(R0, x), one(R1, x), one(R2, x)
                m00 = 0.5 * (r0 + one(R0, jnp.maximum(x - 1, 0)))
                m01 = 0.5 * (r0 + one(R0, jnp.minimum(x + 1, X - 1)))
                m10 = 0.5 * (r1 + pltpu.roll(r1, 1, 0))
                m11 = 0.5 * (r1 + pltpu.roll(r1, WL - 1, 0))
                m20 = jnp.where(lane == 0, 0.0, 0.5 * (r2 + pltpu.roll(r2, 1, 1)))
                m21 = jnp.where(lane == L - 1, 0.0, 0.5 * (r2 + pltpu.roll(r2, L - 1, 1)))

                def g(page, n, part):
                    return g_buf[page, n * ROWS : (n + 1) * ROWS, part]

                lower, upper = slice(0, L), slice(L, 2 * L)
                g00 = g(p + 1, 0, lower) if q == 1 else g(p, 0, upper)
                g01 = g(p + 2, 1, lower) if q == 1 else g(p + 1, 1, upper)
                terms = [
                    (m00, g00),
                    (m01, g01),
                    (m10, g(p + 1, 2, here)),
                    (m11, g(p + 1, 3, here)),
                    (m20, pltpu.roll(g(p + 1, 4, here), 1, 1)),
                    (m21, pltpu.roll(g(p + 1, 5, here), L - 1, 1)),
                ]
                total = src[:, x]
                for m, v in terms:
                    total = total - m[None] * v.reshape(NV, WL, L)
                res[:, x] = total
            return 0

        lax.fori_loop(0, PAIRS, gather, 0)

        @pl.when(at_wall)
        def _():
            def wall_term(x, _):
                res[:, x] = res[:, x] - diag[:, x] * plane3(x)
                return 0

            lax.fori_loop(0, X, wall_term, 0)

    def finish(r, last):
        for side in range(2):
            for half in range(2):
                spread[side, half, pl.ds(2 - side, X, stride=2), :] = recv_p[r, side, half, 0:X, :]
        cols = []
        for side in range(2):
            hi, lo = split(jnp.concatenate([spread[side, 0], spread[side, 1]], axis=1))
            cols += [hi, lo, hi]
        cols = jnp.concatenate(cols, axis=1)
        cols = jnp.concatenate([cols, jnp.zeros((L - 32, cols.shape[1]), BF)], axis=0)
        edge_cols = dot_nt(w_span[...], cols)

        ends = [split(recv_s[r, side].reshape(B1, L)) for side in range(2)]
        g_ends = dot(w_all[0 : 2 * ROWS, :], planes_rhs(ends))
        for side, x in ((0, 0), (1, X - 1)):
            rate = 0.5 * (one(R0, x) + recv_s[r, side, NV])
            g_end = g_ends[side * ROWS : (side + 1) * ROWS, side * L : (side + 1) * L]
            res[:, x] = res[:, x] - rate[None] * g_end.reshape(NV, WL, L)

        for p in range(PAIRS):
            xs = (2 * p, 2 * p + 1)
            rhs = []
            for x in xs:
                rows = jnp.concatenate([recv_w[r, side, pl.ds(x, 24, stride=X), :] for side in range(2)], axis=0)
                rhs.append(stacked(*split(rows), 256))
            g_wall = dot(w_wall[...], jnp.concatenate(rhs, axis=1))
            parts = []
            for q, x in enumerate(xs):
                edge = pltpu.roll(edge_cols, (2 * L - 2 * x - 2) % L, 1)
                if r == 0:
                    r0, r1, r2 = one(R0, x), one(R1, x), one(R2, x)
                    r0m = recv_s[r, 0, NV] if x == 0 else one(R0, x - 1)
                    r0p = recv_s[r, 1, NV] if x == X - 1 else one(R0, x + 1)
                    low = recv_w[r, 0, NV * X + x : NV * X + x + 1, :]
                    high = recv_w[r, 1, NV * X + x : NV * X + x + 1, :]
                    r1m = jnp.where(sub == 0, jnp.broadcast_to(low, (WL, L)), pltpu.roll(r1, 1, 0))
                    r1p = jnp.where(sub == WL - 1, jnp.broadcast_to(high, (WL, L)), pltpu.roll(r1, WL - 1, 0))
                    beyond = edge[ROWS:B1]
                    r2m = jnp.where(lane == 0, beyond, pltpu.roll(r2, 1, 1))
                    r2p = jnp.where(lane == L - 1, beyond, pltpu.roll(r2, L - 1, 1))
                    total = 1.0 + (r0 + r1 + r2) + 0.5 * ((r0m + r0p) + (r1m + r1p) + (r2m + r2p))
                    rate_w = jnp.where(sub == 0, 0.5 * (r1 + r1m), jnp.where(sub == WL - 1, 0.5 * (r1 + r1p), 0.0))
                    rate_s = jnp.where(lane == 0, 0.5 * (r2 + r2m), jnp.where(lane == L - 1, 0.5 * (r2 + r2p), 0.0))
                    rates[x, 0] = total
                    rates[x, 1] = 1.0 / total
                    rates[x, 2] = rate_w
                    rates[x, 3] = rate_s
                total, rate_w, rate_s = rates[x, 0], rates[x, 2], rates[x, 3]
                value = res[:, x] - total[None] * plane3(x)
                value = value - rate_w[None] * g_wall[0:ROWS, q * L : (q + 1) * L].reshape(NV, WL, L)
                value = value - rate_s[None] * edge[0:ROWS].reshape(NV, WL, L)
                if last:
                    res_out[:, x] = value
                value = jnp.concatenate([value.reshape(ROWS, L), jnp.zeros((WL, L), F32)], axis=0)
                parts.append(split(value))
            update = dot(w_p[...], planes_rhs(parts))
            for q, x in enumerate(xs):
                step = update[0:ROWS, q * L : (q + 1) * L].reshape(NV, WL, L)
                value = plane3(x) + step * rates[x, 1][None]
                if last:
                    adj_out[:, x] = value
                else:
                    for j in range(NV):
                        ar[at(j, x), :] = value[j]
                    store_split(x, value.reshape(ROWS, L))

    pack(0)
    pl.semaphore_wait(
        barrier,
        2
        + (st > 0).astype(jnp.int32)
        + (st < n_st - 1).astype(jnp.int32)
        + (wl > 0).astype(jnp.int32)
        + (wl < n_wl - 1).astype(jnp.int32),
    )
    send(0)
    for c in small:
        c.wait()
    build_weights(fc, pinv, w_all, w_p, w_span, w_wall)

    @pl.when(at_wall)
    def _():
        for c in code_loads:
            c.wait()
        tg[...] = jnp.zeros((8, NV), F32)
        tg[0:4, :] = table[...]
        tg[4:5, :] = gain[...]
        own = (iota((ROWS, NV), 0) == WL * iota((ROWS, NV), 1)).astype(F32)
        coef = lax.dot_general(own, tg[...], (((1,), (1,)), ((), ())), precision=HI, preferred_element_type=F32)

        def coef_of(x, _):
            codes = jnp.broadcast_to(code[pl.ds(x + off, 1), :], (8, L))
            spall = jnp.broadcast_to(mask[pl.ds(x + off, 1), :], (8, L))
            hot = jnp.where(sub < 4, (codes == sub).astype(F32), jnp.where(sub == 4, spall.astype(F32), 0.0))
            wall = lax.dot_general(coef, hot, (((1,), (0,)), ((), ())), precision=HI, preferred_element_type=F32)
            diag[:, x] = one(R1, x)[None] * wall.reshape(NV, WL, L)
            return 0

        lax.fori_loop(0, X, coef_of, 0)

    loads[3].wait()
    local()
    receive(0)
    finish(0, False)
    pack(1)
    send(1)
    local()
    receive(1)
    finish(1, True)
    for r in range(2):
        for n, c in enumerate(copies(r)):
            when(ways[n][1], c.wait_send)


def drain(adj, res, adj_out, res_out, sem):
    copies = [pltpu.make_async_copy(adj, adj_out, sem.at[0]), pltpu.make_async_copy(res, res_out, sem.at[1])]
    for c in copies:
        c.start()
    for c in copies:
        c.wait()


def on_device(adj_init, adj_source, velocity, sound, face_couple, precond_inv, wall_code, spall_mask, wall_table, spall_gain):
    field = jax.ShapeDtypeStruct((NV, X, WL, L), F32)
    hbm = pl.BlockSpec(memory_space=pltpu.HBM)
    inside = pl.BlockSpec(memory_space=pltpu.VMEM)
    results = pl.pallas_call(
        kernel,
        out_shape=(field, field),
        in_specs=[hbm] * 10,
        out_specs=(inside, inside),
        scratch_shapes=[
            pltpu.VMEM((20 * X * WL, L), F32),
            pltpu.VMEM((NV, X, WL, L), F32),
            pltpu.VMEM((3, X, WL, L), F32),
            pltpu.VMEM((X, WL, L), F32),
            pltpu.VMEM((16, L), jnp.int32),
            pltpu.VMEM((16, L), jnp.int32),
            pltpu.VMEM((3, NV, 2, NV), F32),
            pltpu.VMEM((NV, NV), F32),
            pltpu.VMEM((4, NV), F32),
            pltpu.VMEM((1, NV), F32),
            pltpu.VMEM((NV, X, WL, L), F32),
            pltpu.VMEM((X, 2, B1, L), BF),
            pltpu.VMEM((PAIRS + 2, 6 * ROWS, 2 * L), F32),
            pltpu.VMEM((NV, X, WL, L), F32),
            pltpu.VMEM((6 * ROWS, 512), BF),
            pltpu.VMEM((B1, 512), BF),
            pltpu.VMEM((B1, 1536), BF),
            pltpu.VMEM((B1, 256), BF),
            pltpu.VMEM((32, 256 * X), BF),
            pltpu.VMEM((8, NV), F32),
            pltpu.VMEM((2, 2, 18, WL, L), F32),
            pltpu.VMEM((2, 2, WROWS, L), F32),
            pltpu.VMEM((2, 2, 2, 16, L), F32),
            pltpu.VMEM((2, 2, 18, WL, L), F32),
            pltpu.VMEM((2, 2, 24 * X, L), F32),
            pltpu.VMEM((2, 2, 2, 16, L), F32),
            pltpu.VMEM((2, 2, 32, L), F32),
            pltpu.VMEM((X, 4, WL, L), F32),
            pltpu.SemaphoreType.DMA((10,)),
            pltpu.SemaphoreType.DMA((2, 6)),
            pltpu.SemaphoreType.DMA((2, 6)),
        ],
        compiler_params=pltpu.CompilerParams(collective_id=0, has_side_effects=True, vmem_limit_bytes=40 * 1024 * 1024),
        name="sweeps",
    )(
        *[
            pltpu.with_memory_space_constraint(v, pltpu.HBM)
            for v in (
                adj_init.reshape(NV * X * WL, L),
                adj_source,
                velocity,
                sound,
                wall_code,
                spall_mask,
                face_couple.transpose(0, 2, 1, 3),
                precond_inv,
                wall_table,
                spall_gain.reshape(1, NV),
            )
        ]
    )
    return pl.pallas_call(
        drain,
        out_shape=(field, field),
        in_specs=[inside] * 2,
        out_specs=(hbm, hbm),
        scratch_shapes=[pltpu.SemaphoreType.DMA((2,))],
        compiler_params=pltpu.CompilerParams(vmem_limit_bytes=40 * 1024 * 1024),
        name="drain",
    )(*results)


def solution(mesh):
    field = P(None, "stream", "wall", "span")
    return jax.shard_map(
        on_device,
        mesh=mesh,
        in_specs=(field, field, field, P("stream", "wall", "span"), P(), P(), P(), P(), P(), P()),
        out_specs=(field, field),
        check_vma=False,
    )
```

```python
import jax
import jax.numpy as jnp
from jax import lax
from jax.experimental import pallas as pl
from jax.experimental.pallas import tpu as pltpu
from jax.sharding import PartitionSpec as P

NV = 17
X = 12
WL = 8
L = 128
B1 = 144
ROWS = NV * WL
PAIRS = X // 2
R1, R0, R2 = 17, 18, 19
WROWS = 18 * X
F32, BF = jnp.float32, jnp.bfloat16
HI = lax.Precision.HIGHEST
MESH = pl.DeviceIdType.MESH


def iota(shape, dim):
    return lax.broadcasted_iota(jnp.int32, shape, dim)


def dot(a, b):
    return lax.dot_general(a, b, (((1,), (0,)), ((), ())), preferred_element_type=F32)


def dot_nt(a, b):
    return lax.dot_general(a, b, (((1,), (1,)), ((), ())), preferred_element_type=F32)


def split(v):
    hi = v.astype(BF)
    return hi, (v - hi.astype(F32)).astype(BF)


def stacked(hi, lo, rows):
    parts = [hi, lo, hi]
    short = rows - 3 * hi.shape[0]
    return jnp.concatenate(parts + [jnp.zeros((short, hi.shape[1]), BF)], axis=0)


def build_weights(fc, pinv, w_all, w_p, w_span, w_wall):
    spread = (iota((B1, NV), 0) // WL == iota((B1, NV), 1)).astype(BF)
    both = [jnp.concatenate(split(fc[d].reshape(2 * NV, NV)), axis=0) for d in range(3)]
    rows = [dot_nt(spread, v).astype(BF) for v in both]
    p_rows = jnp.concatenate([dot(spread, v).astype(BF) for v in split(pinv[...])], axis=1)

    def fold(k, length):
        return jnp.where(k >= 2 * length, k - 2 * length, jnp.where(k >= length, k - length, k))

    def picker(n_rows, width, length, s, low_at):
        js, k = iota((2 * n_rows, width), 0), iota((2 * n_rows, width), 1)
        low = js >= n_rows
        js = jnp.where(low, js - n_rows, js)
        kk = fold(k, length) if length else k
        if s is None:
            return js, k, kk, low == (k >= low_at)
        return js // 2, k, kk, (low == (k >= low_at)) & (js % 2 == s)

    k = iota((B1, 512), 1)
    w = iota((B1, 512), 0) % WL
    wk = fold(k, B1) % WL

    def expand(values, pick, shift):
        return jnp.where(wk == w + shift, dot(values, pick), 0.0)

    picks = []
    for s in range(2):
        j, kc, kk, ok = picker(2 * NV, 512, B1, s, 2 * B1)
        picks.append((ok & (kk // WL == j) & (kc < 3 * B1)).astype(BF))
    for d in range(3):
        shifts = (-1, 1) if d == 1 else (0, 0)
        pair = [expand(rows[d], picks[s], shifts[s])[:ROWS] for s in range(2)]
        w_all[2 * ROWS * d : 2 * ROWS * (d + 1), :] = jnp.concatenate(pair, axis=0).astype(BF)
    j, kc, kk, ok = picker(NV, 512, B1, None, 2 * B1)
    p_pick = (ok & (kk // WL == j) & (kc < 3 * B1)).astype(BF)
    w_p[...] = expand(p_rows, p_pick, 0).astype(BF)

    ks = iota((B1, 512), 1)
    rs = iota((B1, 512), 0)
    kq = jnp.where(ks >= 256, ks - 256, ks)
    same_cell = (rs % WL == kq % WL) & (kq < ROWS)

    for s in range(2):
        j, kc, _, ok = picker(2 * NV, 512, 0, s, 256)
        kk = jnp.where(kc >= 256, kc - 256, kc)
        full = dot(rows[2], (ok & (kk // WL == j)).astype(BF))
        full = jnp.where(same_cell, full, 0.0)
        full = jnp.where((rs >= ROWS) & (rs == ks), 1.0, full).astype(BF)
        w_span[:, 768 * s : 768 * s + 256] = full[:, 0:256]
        w_span[:, 768 * s + 256 : 768 * s + 768] = full

    ks, rs = iota((B1, 256), 1), iota((B1, 256), 0)
    full = 0.0
    for s in range(2):
        j, kc, kk, ok = picker(2 * NV, 256, 48, s, 96)
        part = dot(rows[1], (ok & (kk - 24 * s == j) & (kc < 144)).astype(BF))
        full = full + jnp.where(rs % WL == (WL - 1) * s, part, 0.0)
    w_wall[...] = jnp.where(rs < ROWS, full, 0.0).astype(BF)


def kernel(
    adj_in, src_in, vel_in, snd_in, code_in, mask_in, fc_in, pinv_in, table_in, gain_in,
    adj_out, res_out, t_adj, t_res,
    ar, src, vel, snd, code, mask, fc, pinv, table, gain, res, split_a, g_buf, diag,
    w_all, w_p, w_span, w_wall, tg,
    send_s, send_w, send_p, recv_s, recv_w, recv_p, spread, rates, cols, col_rates,
    in_sem, send_sem, recv_sem,
):
    st, sp, wl = (lax.axis_index(a) for a in ("stream", "span", "wall"))
    n_st, n_sp, n_wl = (lax.axis_size(a) for a in ("stream", "span", "wall"))
    right, left = lax.rem(sp + 1, n_sp), lax.rem(sp + n_sp - 1, n_sp)
    ways = [
        ({"stream": st + 1}, st < n_st - 1, st > 0),
        ({"stream": st - 1}, st > 0, st < n_st - 1),
        ({"wall": wl + 1}, wl < n_wl - 1, wl > 0),
        ({"wall": wl - 1}, wl > 0, wl < n_wl - 1),
        ({"span": right}, None, None),
        ({"span": left}, None, None),
    ]

    def when(cond, fn):
        if cond is None:
            fn()
        else:
            pl.when(cond)(fn)

    barrier = pltpu.get_barrier_semaphore()
    for device, sends, _ in ways:
        when(sends, lambda device=device: pl.semaphore_signal(barrier, inc=1, device_id=device, device_id_type=MESH))

    loads = [
        pltpu.make_async_copy(adj_in, ar.at[0 : NV * X * WL, :], in_sem.at[0]),
        pltpu.make_async_copy(vel_in, vel, in_sem.at[1]),
        pltpu.make_async_copy(snd_in, snd, in_sem.at[2]),
        pltpu.make_async_copy(src_in, src, in_sem.at[3]),
    ]
    small = [
        pltpu.make_async_copy(fc_in, fc, in_sem.at[6]),
        pltpu.make_async_copy(pinv_in, pinv, in_sem.at[7]),
        pltpu.make_async_copy(table_in, table, in_sem.at[8]),
        pltpu.make_async_copy(gain_in, gain, in_sem.at[9]),
    ]
    for c in small + loads:
        c.start()
    row0 = pl.multiple_of(X * st - 4 * lax.rem(st, 2), 8)
    off = 4 * lax.rem(st, 2)
    col0 = pl.multiple_of(L * sp, L)
    at_wall = wl == 0
    code_loads = [
        pltpu.make_async_copy(code_in.at[pl.ds(row0, 16), pl.ds(col0, L)], code, in_sem.at[4]),
        pltpu.make_async_copy(mask_in.at[pl.ds(row0, 16), pl.ds(col0, L)], mask, in_sem.at[5]),
    ]

    @pl.when(at_wall)
    def _():
        for c in code_loads:
            c.start()

    for r in range(2):
        for side in range(2):
            recv_w[r, side, WROWS:, :] = jnp.zeros((recv_w.shape[2] - WROWS, L), F32)
            send_p[r, side] = jnp.zeros((2, 16, L), F32)

            @pl.when(jnp.logical_not(ways[side][2]))
            def _():
                recv_s[r, side] = jnp.zeros((18, WL, L), F32)

            @pl.when(jnp.logical_not(ways[2 + side][2]))
            def _():
                recv_w[r, side, 0:WROWS, :] = jnp.zeros((WROWS, L), F32)

    spread[...] = jnp.zeros((2, 2, 32, L), F32)
    g_buf[0, 0:ROWS, :] = jnp.zeros((ROWS, 2 * L), F32)
    g_buf[PAIRS + 1, ROWS : 2 * ROWS, :] = jnp.zeros((ROWS, 2 * L), F32)
    for c in small:
        c.wait()
    build_weights(fc, pinv, w_all, w_p, w_span, w_wall)

    for c in loads[:3]:
        c.wait()
    for d, slot in ((0, R0), (1, R1), (2, R2)):
        ar[slot * X * WL : (slot + 1) * X * WL, :] = (jnp.abs(vel[d]) + snd[...]).reshape(X * WL, L)

    def at(slot, x):
        start = slot * X * WL + x * WL
        return pl.ds(start if isinstance(start, int) else pl.multiple_of(start, WL), WL)

    def one(slot, x):
        return ar[at(slot, x), :]

    def plane(x):
        return jnp.concatenate([one(j, x) for j in range(NV)], axis=0)

    def plane3(x):
        return plane(x).reshape(NV, WL, L)

    def store_split(x, value, extra):
        hi, lo = split(jnp.concatenate([value, extra], axis=0))
        split_a[x, 0] = hi
        split_a[x, 1] = lo

    def copies(r, which):
        out = []
        for n in which:
            device = ways[n][0]
            bufs = ((send_s, recv_s), (send_w, recv_w), (send_p, recv_p))[n // 2]
            side = n % 2
            if n // 2 == 1:
                dst = bufs[1].at[r, side, 0:WROWS, :]
            else:
                dst = bufs[1].at[r, side]
            out.append(
                pltpu.make_async_remote_copy(
                    src_ref=bufs[0].at[r, side],
                    dst_ref=dst,
                    send_sem=send_sem.at[r, n],
                    recv_sem=recv_sem.at[r, n],
                    device_id=device,
                    device_id_type=MESH,
                )
            )
        return out

    lanes3 = iota((B1, L), 1)
    pick_row, pick_col = iota((32, 2 * L), 0), iota((32, 2 * L), 1) % L
    pick_col = jnp.where(pick_row < 16, pick_col - 2 * pick_row - 1, pick_col - 2 * (pick_row - 16) - 2)
    pick_cols = ((pick_col == 0) & (pick_row % 16 < X)).astype(BF)

    def collect(x, value, into):
        moved = pltpu.roll(value, 2 * x + 2, 1)
        return jnp.where((lanes3 == 2 * x + 1) | (lanes3 == 2 * x + 2), moved, into)

    def to_rows(value):
        return dot_nt(pick_cols, jnp.concatenate(split(value), axis=1))

    def put_columns(r, value):
        for side in range(2):
            send_p[r, side, 0] = value[16 * side : 16 * side + 16, 0:L]
            send_p[r, side, 1, :, 0 : B1 - L] = value[16 * side : 16 * side + 16, L:B1]

    def pack(r):
        for side, w in ((0, WL - 1), (1, 0)):
            send_w[r, side] = ar[pl.ds(w, WROWS, stride=WL), :]
        for side, x in ((0, X - 1), (1, 0)):
            send_s[r, side, 0:NV] = plane3(x)
            send_s[r, side, NV] = one(R0, x)

    near, far = range(4), range(4, 6)

    def send(r, which):
        for n, c in zip(which, copies(r, which)):
            when(ways[n][1], c.start)

    def receive(r, which):
        for n, c in zip(which, copies(r, which)):
            when(ways[n][2], c.wait_recv)

    lane = iota((WL, L), 1)
    sub = iota((WL, L), 0)
    edge_lane = (lane == 0) | (lane == L - 1)

    def planes_rhs(hi_lo_pairs):
        return jnp.concatenate([stacked(h, l, 512) for h, l in hi_lo_pairs], axis=1)

    def local():
        def couple(p, _):
            rhs = planes_rhs([(split_a[2 * p + q, 0], split_a[2 * p + q, 1]) for q in range(2)])
            g_buf[p + 1] = dot(w_all[...], rhs)
            return 0

        lax.fori_loop(0, PAIRS, couple, 0)

        def gather(p, _):
            for q in range(2):
                x = 2 * p + q
                here = slice(q * L, (q + 1) * L)
                r0, r1, r2 = one(R0, x), one(R1, x), one(R2, x)
                m00 = 0.5 * (r0 + one(R0, jnp.maximum(x - 1, 0)))
                m01 = 0.5 * (r0 + one(R0, jnp.minimum(x + 1, X - 1)))
                m10 = 0.5 * (r1 + pltpu.roll(r1, 1, 0))
                m11 = 0.5 * (r1 + pltpu.roll(r1, WL - 1, 0))
                m20 = jnp.where(lane == 0, 0.0, 0.5 * (r2 + pltpu.roll(r2, 1, 1)))
                m21 = jnp.where(lane == L - 1, 0.0, 0.5 * (r2 + pltpu.roll(r2, L - 1, 1)))

                def g(page, n, part):
                    return g_buf[page, n * ROWS : (n + 1) * ROWS, part]

                lower, upper = slice(0, L), slice(L, 2 * L)
                g00 = g(p + 1, 0, lower) if q == 1 else g(p, 0, upper)
                g01 = g(p + 2, 1, lower) if q == 1 else g(p + 1, 1, upper)
                terms = [
                    (m00, g00),
                    (m01, g01),
                    (m10, g(p + 1, 2, here)),
                    (m11, g(p + 1, 3, here)),
                    (m20, pltpu.roll(g(p + 1, 4, here), 1, 1)),
                    (m21, pltpu.roll(g(p + 1, 5, here), L - 1, 1)),
                ]
                total = src[:, x]
                for m, v in terms:
                    total = total - m[None] * v.reshape(NV, WL, L)
                res[:, x] = total
            return 0

        lax.fori_loop(0, PAIRS, gather, 0)

        @pl.when(at_wall)
        def _():
            def wall_term(x, _):
                res[:, x] = res[:, x] - diag[:, x] * plane3(x)
                return 0

            lax.fori_loop(0, X, wall_term, 0)

    def finish(r, last):
        ends = [split(recv_s[r, side].reshape(B1, L)) for side in range(2)]
        g_ends = dot(w_all[0 : 2 * ROWS, :], planes_rhs(ends))
        for side, x in ((0, 0), (1, X - 1)):
            rate = 0.5 * (one(R0, x) + recv_s[r, side, NV])
            g_end = g_ends[side * ROWS : (side + 1) * ROWS, side * L : (side + 1) * L]
            res[:, x] = res[:, x] - rate[None] * g_end.reshape(NV, WL, L)

        columns = jnp.zeros((B1, L), F32)
        for p in range(PAIRS):
            xs = (2 * p, 2 * p + 1)
            rhs = []
            for x in xs:
                rows = jnp.concatenate([recv_w[r, side, pl.ds(x, 24, stride=X), :] for side in range(2)], axis=0)
                rhs.append(stacked(*split(rows), 256))
            g_wall = dot(w_wall[...], jnp.concatenate(rhs, axis=1))
            parts = []
            for q, x in enumerate(xs):
                if r == 0:
                    r0, r1, r2 = one(R0, x), one(R1, x), one(R2, x)
                    r0m = recv_s[r, 0, NV] if x == 0 else one(R0, x - 1)
                    r0p = recv_s[r, 1, NV] if x == X - 1 else one(R0, x + 1)
                    low = recv_w[r, 0, NV * X + x : NV * X + x + 1, :]
                    high = recv_w[r, 1, NV * X + x : NV * X + x + 1, :]
                    r1m = jnp.where(sub == 0, jnp.broadcast_to(low, (WL, L)), pltpu.roll(r1, 1, 0))
                    r1p = jnp.where(sub == WL - 1, jnp.broadcast_to(high, (WL, L)), pltpu.roll(r1, WL - 1, 0))
                    r2m = jnp.where(lane == 0, 0.0, pltpu.roll(r2, 1, 1))
                    r2p = jnp.where(lane == L - 1, 0.0, pltpu.roll(r2, L - 1, 1))
                    total = 1.0 + (r0 + r1 + r2) + 0.5 * ((r0m + r0p) + (r1m + r1p) + (r2m + r2p))
                    rates[x, 0] = total
                    rates[x, 1] = 1.0 / total
                    rates[x, 2] = jnp.where(sub == 0, 0.5 * (r1 + r1m), jnp.where(sub == WL - 1, 0.5 * (r1 + r1p), 0.0))
                total, rate_w = rates[x, 0], rates[x, 2]
                value = res[:, x] - total[None] * plane3(x)
                value = value - rate_w[None] * g_wall[0:ROWS, q * L : (q + 1) * L].reshape(NV, WL, L)
                if last:
                    res_out[:, x] = value
                value = jnp.concatenate([value.reshape(ROWS, L), jnp.zeros((WL, L), F32)], axis=0)
                parts.append(split(value))
            update = dot(w_p[...], planes_rhs(parts))
            for q, x in enumerate(xs):
                step = update[0:ROWS, q * L : (q + 1) * L].reshape(NV, WL, L)
                value = plane3(x) + step * rates[x, 1][None]
                if last:
                    adj_out[:, x] = value
                else:
                    for j in range(NV):
                        ar[at(j, x), :] = value[j]
                    step = jnp.concatenate([step.reshape(ROWS, L), rates[x, 0]], axis=0)
                    columns = collect(x, step, columns)
        if not last:
            cols[1] = columns

    def edges(r):
        halo = []
        for side in range(2):
            for half in range(2):
                spread[side, half, pl.ds(2 - side, X, stride=2), :] = recv_p[r, side, half, 0:X, :]
            hi, lo = split(jnp.concatenate([spread[side, 0], spread[side, 1]], axis=1))
            halo += [hi, lo, hi]
        halo = jnp.concatenate(halo, axis=1)
        halo = jnp.concatenate([halo, jnp.zeros((L - 32, halo.shape[1]), BF)], axis=0)
        halo = dot_nt(w_span[...], halo)
        flow = halo[0:ROWS].reshape(NV, WL, L)
        if r == 0:
            beyond = halo[ROWS:B1]
            total = cols[1, ROWS:B1, :] + 0.5 * beyond
            rate = 0.5 * (cols[0, ROWS:B1, :] + beyond)
            used = (lane >= 1) & (lane <= 2 * X)
            total = jnp.where(used, total, 1.0)
            inverse = 1.0 / total
            col_rates[0] = rate
            col_rates[1] = inverse
            before = cols[0, 0:ROWS, :].reshape(NV, WL, L)
            change = -(0.5 * beyond)[None] * before - rate[None] * flow
        else:
            inverse = col_rates[1]
            change = -col_rates[0][None] * flow
        change = jnp.concatenate([change.reshape(ROWS, L), jnp.zeros((WL, L), F32)], axis=0)
        moved = dot(w_p[...], stacked(*split(change), 512))
        moved = moved[0:ROWS].reshape(NV, WL, L)
        if r == 0:
            update = cols[1, 0:ROWS, :].reshape(NV, WL, L) + moved
            value = before + update * inverse[None]
            return jnp.concatenate([value.reshape(ROWS, L), total], axis=0)
        return change, jnp.concatenate([(moved * inverse[None]).reshape(ROWS, L), jnp.zeros((WL, L), F32)], axis=0)

    def apply(turned):
        for x in range(X):
            edge = pltpu.roll(turned, edge_turn(x), 1)
            value = jnp.where(edge_lane[None], edge[0:ROWS].reshape(NV, WL, L), plane3(x))
            total = jnp.where(edge_lane, edge[ROWS:B1], rates[x, 0])
            rates[x, 0] = total
            rates[x, 1] = 1.0 / total
            for j in range(NV):
                ar[at(j, x), :] = value[j]
            store_split(x, value.reshape(ROWS, L), total)

    columns = jnp.zeros((B1, L), F32)
    for x in range(X):
        value = plane(x)
        store_split(x, value, one(R2, x))
        columns = collect(x, jnp.concatenate([value, one(R2, x)], axis=0), columns)
    put_columns(0, to_rows(columns))
    cols[0] = columns
    pack(0)
    pl.semaphore_wait(
        barrier,
        2
        + (st > 0).astype(jnp.int32)
        + (st < n_st - 1).astype(jnp.int32)
        + (wl > 0).astype(jnp.int32)
        + (wl < n_wl - 1).astype(jnp.int32),
    )
    send(0, far)
    send(0, near)

    @pl.when(at_wall)
    def _():
        for c in code_loads:
            c.wait()
        tg[...] = jnp.zeros((8, NV), F32)
        tg[0:4, :] = table[...]
        tg[4:5, :] = gain[...]
        own = (iota((ROWS, NV), 0) == WL * iota((ROWS, NV), 1)).astype(F32)
        coef = lax.dot_general(own, tg[...], (((1,), (1,)), ((), ())), precision=HI, preferred_element_type=F32)

        def coef_of(x, _):
            codes = jnp.broadcast_to(code[pl.ds(x + off, 1), :], (8, L))
            spall = jnp.broadcast_to(mask[pl.ds(x + off, 1), :], (8, L))
            hot = jnp.where(sub < 4, (codes == sub).astype(F32), jnp.where(sub == 4, spall.astype(F32), 0.0))
            wall = lax.dot_general(coef, hot, (((1,), (0,)), ((), ())), precision=HI, preferred_element_type=F32)
            diag[:, x] = one(R1, x)[None] * wall.reshape(NV, WL, L)
            return 0

        lax.fori_loop(0, X, coef_of, 0)

    loads[3].wait()
    local()
    receive(0, near)
    finish(0, False)
    receive(0, far)
    edge_adj = edges(0)
    put_columns(1, to_rows(edge_adj))
    send(1, far)
    apply(edge_adj)
    pack(1)
    send(1, near)
    local()
    receive(1, near)
    finish(1, True)
    receive(1, far)
    t_res[...], t_adj[...] = edges(1)
    for r in range(2):
        for n, c in enumerate(copies(r, range(6))):
            when(ways[n][1], c.wait_send)


def edge_turn(x):
    return (2 * L - 2 * x - 2) % L


def drain(adj, res, t_adj, t_res, adj_out, res_out, adj_buf, res_buf, sem):
    lane = iota((WL, L), 1)
    edge_lane = ((lane == 0) | (lane == L - 1))[None]
    copies = []
    for p in range(PAIRS):
        part = pl.ds(2 * p, 2)
        for n, (field, turned, buf, out) in enumerate(((adj, t_adj, adj_buf, adj_out), (res, t_res, res_buf, res_out))):
            for x in (2 * p, 2 * p + 1):
                edge = pltpu.roll(turned[0:ROWS, :], edge_turn(x), 1).reshape(NV, WL, L)
                buf[:, x] = field[:, x] + jnp.where(edge_lane, edge, 0.0)
            copy = pltpu.make_async_copy(buf.at[:, part], out.at[:, part], sem.at[n, p])
            copy.start()
            copies.append(copy)
    for c in copies:
        c.wait()


def on_device(adj_init, adj_source, velocity, sound, face_couple, precond_inv, wall_code, spall_mask, wall_table, spall_gain):
    field = jax.ShapeDtypeStruct((NV, X, WL, L), F32)
    turned = jax.ShapeDtypeStruct((B1, L), F32)
    hbm = pl.BlockSpec(memory_space=pltpu.HBM)
    inside = pl.BlockSpec(memory_space=pltpu.VMEM)
    results = pl.pallas_call(
        kernel,
        out_shape=(field, field, turned, turned),
        in_specs=[hbm] * 10,
        out_specs=(inside,) * 4,
        scratch_shapes=[
            pltpu.VMEM((20 * X * WL, L), F32),
            pltpu.VMEM((NV, X, WL, L), F32),
            pltpu.VMEM((3, X, WL, L), F32),
            pltpu.VMEM((X, WL, L), F32),
            pltpu.VMEM((16, L), jnp.int32),
            pltpu.VMEM((16, L), jnp.int32),
            pltpu.VMEM((3, NV, 2, NV), F32),
            pltpu.VMEM((NV, NV), F32),
            pltpu.VMEM((4, NV), F32),
            pltpu.VMEM((1, NV), F32),
            pltpu.VMEM((NV, X, WL, L), F32),
            pltpu.VMEM((X, 2, B1, L), BF),
            pltpu.VMEM((PAIRS + 2, 6 * ROWS, 2 * L), F32),
            pltpu.VMEM((NV, X, WL, L), F32),
            pltpu.VMEM((6 * ROWS, 512), BF),
            pltpu.VMEM((B1, 512), BF),
            pltpu.VMEM((B1, 1536), BF),
            pltpu.VMEM((B1, 256), BF),
            pltpu.VMEM((8, NV), F32),
            pltpu.VMEM((2, 2, 18, WL, L), F32),
            pltpu.VMEM((2, 2, WROWS, L), F32),
            pltpu.VMEM((2, 2, 2, 16, L), F32),
            pltpu.VMEM((2, 2, 18, WL, L), F32),
            pltpu.VMEM((2, 2, 24 * X, L), F32),
            pltpu.VMEM((2, 2, 2, 16, L), F32),
            pltpu.VMEM((2, 2, 32, L), F32),
            pltpu.VMEM((X, 4, WL, L), F32),
            pltpu.VMEM((2, B1, L), F32),
            pltpu.VMEM((2, WL, L), F32),
            pltpu.SemaphoreType.DMA((10,)),
            pltpu.SemaphoreType.DMA((2, 6)),
            pltpu.SemaphoreType.DMA((2, 6)),
        ],
        compiler_params=pltpu.CompilerParams(collective_id=0, has_side_effects=True, vmem_limit_bytes=40 * 1024 * 1024),
        name="sweeps",
    )(
        *[
            pltpu.with_memory_space_constraint(v, pltpu.HBM)
            for v in (
                adj_init.reshape(NV * X * WL, L),
                adj_source,
                velocity,
                sound,
                wall_code,
                spall_mask,
                face_couple.transpose(0, 2, 1, 3),
                precond_inv,
                wall_table,
                spall_gain.reshape(1, NV),
            )
        ]
    )
    return pl.pallas_call(
        drain,
        out_shape=(field, field),
        in_specs=[inside] * 4,
        out_specs=(hbm, hbm),
        scratch_shapes=[
            pltpu.VMEM((NV, X, WL, L), F32),
            pltpu.VMEM((NV, X, WL, L), F32),
            pltpu.SemaphoreType.DMA((2, PAIRS)),
        ],
        compiler_params=pltpu.CompilerParams(vmem_limit_bytes=40 * 1024 * 1024),
        name="drain",
    )(*results)


def solution(mesh):
    field = P(None, "stream", "wall", "span")
    return jax.shard_map(
        on_device,
        mesh=mesh,
        in_specs=(field, field, field, P("stream", "wall", "span"), P(), P(), P(), P(), P(), P()),
        out_specs=(field, field),
        check_vma=False,
    )
```

```python
import jax
import jax.numpy as jnp
from jax import lax
from jax.experimental import pallas as pl
from jax.experimental.pallas import tpu as pltpu
from jax.sharding import PartitionSpec as P

NV = 17
X = 12
WL = 8
L = 128
B1 = 144
ROWS = NV * WL
PAIRS = X // 2
R1, R0, R2 = 17, 18, 19
WROWS = 18 * X
F32, BF = jnp.float32, jnp.bfloat16
HI = lax.Precision.HIGHEST
MESH = pl.DeviceIdType.MESH


def iota(shape, dim):
    return lax.broadcasted_iota(jnp.int32, shape, dim)


def dot(a, b):
    return lax.dot_general(a, b, (((1,), (0,)), ((), ())), preferred_element_type=F32)


def dot_nt(a, b):
    return lax.dot_general(a, b, (((1,), (1,)), ((), ())), preferred_element_type=F32)


def split(v):
    hi = v.astype(BF)
    return hi, (v - hi.astype(F32)).astype(BF)


def stacked(hi, lo, rows):
    parts = [hi, lo, hi]
    short = rows - 3 * hi.shape[0]
    return jnp.concatenate(parts + [jnp.zeros((short, hi.shape[1]), BF)], axis=0)


def build_weights(fc, pinv, w_all, w_p, w_span, w_wall):
    spread = (iota((B1, NV), 0) // WL == iota((B1, NV), 1)).astype(BF)
    both = [jnp.concatenate(split(fc[d].reshape(2 * NV, NV)), axis=0) for d in range(3)]
    rows = [dot_nt(spread, v).astype(BF) for v in both]
    p_rows = jnp.concatenate([dot(spread, v).astype(BF) for v in split(pinv[...])], axis=1)

    def fold(k, length):
        return jnp.where(k >= 2 * length, k - 2 * length, jnp.where(k >= length, k - length, k))

    def picker(n_rows, width, length, s, low_at):
        js, k = iota((2 * n_rows, width), 0), iota((2 * n_rows, width), 1)
        low = js >= n_rows
        js = jnp.where(low, js - n_rows, js)
        kk = fold(k, length) if length else k
        if s is None:
            return js, k, kk, low == (k >= low_at)
        return js // 2, k, kk, (low == (k >= low_at)) & (js % 2 == s)

    k = iota((B1, 512), 1)
    w = iota((B1, 512), 0) % WL
    wk = fold(k, B1) % WL

    def expand(values, pick, shift):
        return jnp.where(wk == w + shift, dot(values, pick), 0.0)

    picks = []
    for s in range(2):
        j, kc, kk, ok = picker(2 * NV, 512, B1, s, 2 * B1)
        picks.append((ok & (kk // WL == j) & (kc < 3 * B1)).astype(BF))
    for d in range(3):
        shifts = (-1, 1) if d == 1 else (0, 0)
        pair = [expand(rows[d], picks[s], shifts[s])[:ROWS] for s in range(2)]
        w_all[2 * ROWS * d : 2 * ROWS * (d + 1), :] = jnp.concatenate(pair, axis=0).astype(BF)
    j, kc, kk, ok = picker(NV, 512, B1, None, 2 * B1)
    p_pick = (ok & (kk // WL == j) & (kc < 3 * B1)).astype(BF)
    w_p[...] = expand(p_rows, p_pick, 0).astype(BF)

    ks = iota((B1, 512), 1)
    rs = iota((B1, 512), 0)
    kq = jnp.where(ks >= 256, ks - 256, ks)
    same_cell = (rs % WL == kq % WL) & (kq < ROWS)

    for s in range(2):
        j, kc, _, ok = picker(2 * NV, 512, 0, s, 256)
        kk = jnp.where(kc >= 256, kc - 256, kc)
        full = dot(rows[2], (ok & (kk // WL == j)).astype(BF))
        full = jnp.where(same_cell, full, 0.0)
        full = jnp.where((rs >= ROWS) & (rs == ks), 1.0, full).astype(BF)
        w_span[B1 * s : B1 * (s + 1), 0:256] = full[:, 0:256]
        w_span[B1 * s : B1 * (s + 1), 256:768] = full

    ks, rs = iota((B1, 256), 1), iota((B1, 256), 0)
    full = 0.0
    for s in range(2):
        j, kc, kk, ok = picker(2 * NV, 256, 48, s, 96)
        part = dot(rows[1], (ok & (kk - 24 * s == j) & (kc < 144)).astype(BF))
        full = full + jnp.where(rs % WL == (WL - 1) * s, part, 0.0)
    w_wall[...] = jnp.where(rs < ROWS, full, 0.0).astype(BF)


def kernel(
    adj_in, src_in, vel_in, snd_in, code_in, mask_in, fc_in, pinv_in, table_in, gain_in,
    adj_out, res_out, t_adj, t_res,
    ar, src, vel, snd, code, mask, fc, pinv, table, gain, res, split_a, g_buf, diag,
    w_all, w_p, w_span, w_wall, tg,
    send_s, send_w, send_p, recv_s, recv_w, recv_p, spread, rates, cols, col_rates,
    in_sem, send_sem, recv_sem,
):
    st, sp, wl = (lax.axis_index(a) for a in ("stream", "span", "wall"))
    n_st, n_sp, n_wl = (lax.axis_size(a) for a in ("stream", "span", "wall"))
    right, left = lax.rem(sp + 1, n_sp), lax.rem(sp + n_sp - 1, n_sp)
    ways = [
        ({"stream": st + 1}, st < n_st - 1, st > 0),
        ({"stream": st - 1}, st > 0, st < n_st - 1),
        ({"wall": wl + 1}, wl < n_wl - 1, wl > 0),
        ({"wall": wl - 1}, wl > 0, wl < n_wl - 1),
        ({"span": right}, None, None),
        ({"span": left}, None, None),
    ]

    def when(cond, fn):
        if cond is None:
            fn()
        else:
            pl.when(cond)(fn)

    barrier = pltpu.get_barrier_semaphore()
    for device, sends, _ in ways[4:] + ways[:4]:
        when(sends, lambda device=device: pl.semaphore_signal(barrier, inc=1, device_id=device, device_id_type=MESH))

    loads = [
        pltpu.make_async_copy(adj_in, ar.at[0 : NV * X * WL, :], in_sem.at[0]),
        pltpu.make_async_copy(vel_in, vel, in_sem.at[1]),
        pltpu.make_async_copy(snd_in, snd, in_sem.at[2]),
        pltpu.make_async_copy(src_in, src, in_sem.at[3]),
    ]
    small = [
        pltpu.make_async_copy(fc_in, fc, in_sem.at[6]),
        pltpu.make_async_copy(pinv_in, pinv, in_sem.at[7]),
        pltpu.make_async_copy(table_in, table, in_sem.at[8]),
        pltpu.make_async_copy(gain_in, gain, in_sem.at[9]),
    ]
    for c in small + loads:
        c.start()
    row0 = pl.multiple_of(X * st - 4 * lax.rem(st, 2), 8)
    off = 4 * lax.rem(st, 2)
    col0 = pl.multiple_of(L * sp, L)
    at_wall = wl == 0
    code_loads = [
        pltpu.make_async_copy(code_in.at[pl.ds(row0, 16), pl.ds(col0, L)], code, in_sem.at[4]),
        pltpu.make_async_copy(mask_in.at[pl.ds(row0, 16), pl.ds(col0, L)], mask, in_sem.at[5]),
    ]

    @pl.when(at_wall)
    def _():
        for c in code_loads:
            c.start()

    for r in range(2):
        for side in range(2):
            recv_w[r, side, WROWS:, :] = jnp.zeros((recv_w.shape[2] - WROWS, L), F32)
            send_p[r, side] = jnp.zeros((2, 16, L), F32)

            @pl.when(jnp.logical_not(ways[side][2]))
            def _():
                recv_s[r, side] = jnp.zeros((18, WL, L), F32)

            @pl.when(jnp.logical_not(ways[2 + side][2]))
            def _():
                recv_w[r, side, 0:WROWS, :] = jnp.zeros((WROWS, L), F32)

    spread[...] = jnp.zeros((2, 32, L), F32)
    g_buf[0, 0:ROWS, :] = jnp.zeros((ROWS, 2 * L), F32)
    g_buf[PAIRS + 1, ROWS : 2 * ROWS, :] = jnp.zeros((ROWS, 2 * L), F32)
    for c in small:
        c.wait()
    build_weights(fc, pinv, w_all, w_p, w_span, w_wall)

    for c in loads[:3]:
        c.wait()
    for d, slot in ((0, R0), (1, R1), (2, R2)):
        ar[slot * X * WL : (slot + 1) * X * WL, :] = (jnp.abs(vel[d]) + snd[...]).reshape(X * WL, L)

    def at(slot, x):
        start = slot * X * WL + x * WL
        return pl.ds(start if isinstance(start, int) else pl.multiple_of(start, WL), WL)

    def one(slot, x):
        return ar[at(slot, x), :]

    def plane(x):
        return jnp.concatenate([one(j, x) for j in range(NV)], axis=0)

    def plane3(x):
        return plane(x).reshape(NV, WL, L)

    def store_split(x, value, extra):
        hi, lo = split(jnp.concatenate([value, extra], axis=0))
        split_a[x, 0] = hi
        split_a[x, 1] = lo

    def copies(r, which):
        out = []
        for n in which:
            device = ways[n][0]
            bufs = ((send_s, recv_s), (send_w, recv_w), (send_p, recv_p))[n // 2]
            side = n % 2
            if n // 2 == 1:
                dst = bufs[1].at[r, side, 0:WROWS, :]
            else:
                dst = bufs[1].at[r, side]
            out.append(
                pltpu.make_async_remote_copy(
                    src_ref=bufs[0].at[r, side],
                    dst_ref=dst,
                    send_sem=send_sem.at[r, n],
                    recv_sem=recv_sem.at[r, n],
                    device_id=device,
                    device_id_type=MESH,
                )
            )
        return out

    lanes3 = iota((B1, L), 1)
    pick_row, pick_col = iota((32, 2 * L), 0), iota((32, 2 * L), 1) % L
    pick_col = jnp.where(pick_row < 16, pick_col - 2 * pick_row - 1, pick_col - 2 * (pick_row - 16) - 2)
    pick_cols = ((pick_col == 0) & (pick_row % 16 < X)).astype(BF)

    def collect(x, value, into):
        moved = pltpu.roll(value, 2 * x + 2, 1)
        return jnp.where((lanes3 == 2 * x + 1) | (lanes3 == 2 * x + 2), moved, into)

    def to_rows(value):
        return dot_nt(pick_cols, jnp.concatenate(split(value), axis=1))

    def put_columns(r, value):
        for side in range(2):
            send_p[r, side, 0] = value[16 * side : 16 * side + 16, 0:L]
            send_p[r, side, 1, :, 0 : B1 - L] = value[16 * side : 16 * side + 16, L:B1]

    def pack(r):
        for side, w in ((0, WL - 1), (1, 0)):
            send_w[r, side] = ar[pl.ds(w, WROWS, stride=WL), :]
        for side, x in ((0, X - 1), (1, 0)):
            send_s[r, side, 0:NV] = plane3(x)
            send_s[r, side, NV] = one(R0, x)

    near, far = range(4), range(4, 6)

    def send(r, which):
        for n, c in zip(which, copies(r, which)):
            when(ways[n][1], c.start)

    def receive(r, which):
        for n, c in zip(which, copies(r, which)):
            when(ways[n][2], c.wait_recv)

    lane = iota((WL, L), 1)
    sub = iota((WL, L), 0)
    edge_lane = (lane == 0) | (lane == L - 1)

    def planes_rhs(hi_lo_pairs):
        return jnp.concatenate([stacked(h, l, 512) for h, l in hi_lo_pairs], axis=1)

    def local():
        def couple(p, _):
            rhs = planes_rhs([(split_a[2 * p + q, 0], split_a[2 * p + q, 1]) for q in range(2)])
            g_buf[p + 1] = dot(w_all[...], rhs)

        def gather(p, _):
            for q in range(2):
                x = 2 * p + q
                here = slice(q * L, (q + 1) * L)
                r0, r1, r2 = one(R0, x), one(R1, x), one(R2, x)
                m00 = 0.5 * (r0 + one(R0, max(x - 1, 0)))
                m01 = 0.5 * (r0 + one(R0, min(x + 1, X - 1)))
                m10 = 0.5 * (r1 + pltpu.roll(r1, 1, 0))
                m11 = 0.5 * (r1 + pltpu.roll(r1, WL - 1, 0))
                m20 = jnp.where(lane == 0, 0.0, 0.5 * (r2 + pltpu.roll(r2, 1, 1)))
                m21 = jnp.where(lane == L - 1, 0.0, 0.5 * (r2 + pltpu.roll(r2, L - 1, 1)))

                def g(page, n, part):
                    return g_buf[page, n * ROWS : (n + 1) * ROWS, part]

                lower, upper = slice(0, L), slice(L, 2 * L)
                g00 = g(p + 1, 0, lower) if q == 1 else g(p, 0, upper)
                g01 = g(p + 2, 1, lower) if q == 1 else g(p + 1, 1, upper)
                terms = [
                    (m00, g00),
                    (m01, g01),
                    (m10, g(p + 1, 2, here)),
                    (m11, g(p + 1, 3, here)),
                    (m20, pltpu.roll(g(p + 1, 4, here), 1, 1)),
                    (m21, pltpu.roll(g(p + 1, 5, here), L - 1, 1)),
                ]
                total = src[:, x]
                for m, v in terms:
                    total = total - m[None] * v.reshape(NV, WL, L)
                res[:, x] = total

        for p in range(PAIRS + 1):
            if p < PAIRS:
                couple(p, 0)
            if p > 0:
                gather(p - 1, 0)

        @pl.when(at_wall)
        def _():
            def wall_term(x, _):
                res[:, x] = res[:, x] - diag[:, x] * plane3(x)
                return 0

            lax.fori_loop(0, X, wall_term, 0)

    def finish(r, last):
        ends = [split(recv_s[r, side].reshape(B1, L)) for side in range(2)]
        g_ends = dot(w_all[0 : 2 * ROWS, :], planes_rhs(ends))
        for side, x in ((0, 0), (1, X - 1)):
            rate = 0.5 * (one(R0, x) + recv_s[r, side, NV])
            g_end = g_ends[side * ROWS : (side + 1) * ROWS, side * L : (side + 1) * L]
            res[:, x] = res[:, x] - rate[None] * g_end.reshape(NV, WL, L)

        columns = jnp.zeros((B1, L), F32)
        for p in range(PAIRS):
            xs = (2 * p, 2 * p + 1)
            rhs = []
            for x in xs:
                rows = jnp.concatenate([recv_w[r, side, pl.ds(x, 24, stride=X), :] for side in range(2)], axis=0)
                rhs.append(stacked(*split(rows), 256))
            g_wall = dot(w_wall[...], jnp.concatenate(rhs, axis=1))
            parts = []
            for q, x in enumerate(xs):
                if r == 0:
                    r0, r1, r2 = one(R0, x), one(R1, x), one(R2, x)
                    r0m = recv_s[r, 0, NV] if x == 0 else one(R0, x - 1)
                    r0p = recv_s[r, 1, NV] if x == X - 1 else one(R0, x + 1)
                    low = recv_w[r, 0, NV * X + x : NV * X + x + 1, :]
                    high = recv_w[r, 1, NV * X + x : NV * X + x + 1, :]
                    r1m = jnp.where(sub == 0, jnp.broadcast_to(low, (WL, L)), pltpu.roll(r1, 1, 0))
                    r1p = jnp.where(sub == WL - 1, jnp.broadcast_to(high, (WL, L)), pltpu.roll(r1, WL - 1, 0))
                    r2m = jnp.where(lane == 0, 0.0, pltpu.roll(r2, 1, 1))
                    r2p = jnp.where(lane == L - 1, 0.0, pltpu.roll(r2, L - 1, 1))
                    total = 1.0 + (r0 + r1 + r2) + 0.5 * ((r0m + r0p) + (r1m + r1p) + (r2m + r2p))
                    rates[x, 0] = total
                    rates[x, 1] = 1.0 / total
                    rates[x, 2] = jnp.where(sub == 0, 0.5 * (r1 + r1m), jnp.where(sub == WL - 1, 0.5 * (r1 + r1p), 0.0))
                total, rate_w = rates[x, 0], rates[x, 2]
                value = res[:, x] - total[None] * plane3(x)
                value = value - rate_w[None] * g_wall[0:ROWS, q * L : (q + 1) * L].reshape(NV, WL, L)
                if last:
                    res_out[:, x] = value
                value = jnp.concatenate([value.reshape(ROWS, L), jnp.zeros((WL, L), F32)], axis=0)
                parts.append(split(value))
            update = dot(w_p[...], planes_rhs(parts))
            for q, x in enumerate(xs):
                step = update[0:ROWS, q * L : (q + 1) * L].reshape(NV, WL, L)
                value = plane3(x) + step * rates[x, 1][None]
                if last:
                    adj_out[:, x] = value
                else:
                    for j in range(NV):
                        ar[at(j, x), :] = value[j]
                    step = jnp.concatenate([step.reshape(ROWS, L), rates[x, 0]], axis=0)
                    columns = collect(x, step, columns)
        if not last:
            cols[1] = columns

    def edges(r):
        for side in range(2):
            for half in range(2):
                spread[half, pl.ds(2 - side, X, stride=2), :] = recv_p[r, side, half, 0:X, :]
        hi, lo = split(jnp.concatenate([spread[0], spread[1]], axis=1))
        halo = jnp.concatenate([hi, lo, hi], axis=1)
        halo = jnp.concatenate([halo, jnp.zeros((L - 32, halo.shape[1]), BF)], axis=0)
        halo = dot_nt(w_span[...], halo)
        halo = jnp.where(lanes3 % 2 == 0, halo[0:B1], halo[B1 : 2 * B1])
        flow = halo[0:ROWS].reshape(NV, WL, L)
        if r == 0:
            beyond = halo[ROWS:B1]
            total = cols[1, ROWS:B1, :] + 0.5 * beyond
            rate = 0.5 * (cols[0, ROWS:B1, :] + beyond)
            used = (lane >= 1) & (lane <= 2 * X)
            total = jnp.where(used, total, 1.0)
            inverse = 1.0 / total
            col_rates[0] = rate
            col_rates[1] = inverse
            before = cols[0, 0:ROWS, :].reshape(NV, WL, L)
            change = -(0.5 * beyond)[None] * before - rate[None] * flow
        else:
            inverse = col_rates[1]
            change = -col_rates[0][None] * flow
        change = jnp.concatenate([change.reshape(ROWS, L), jnp.zeros((WL, L), F32)], axis=0)
        moved = dot(w_p[...], stacked(*split(change), 512))
        moved = moved[0:ROWS].reshape(NV, WL, L)
        if r == 0:
            update = cols[1, 0:ROWS, :].reshape(NV, WL, L) + moved
            value = before + update * inverse[None]
            return jnp.concatenate([value.reshape(ROWS, L), total], axis=0)
        return change, jnp.concatenate([(moved * inverse[None]).reshape(ROWS, L), jnp.zeros((WL, L), F32)], axis=0)

    def apply(turned):
        for x in range(X):
            edge = pltpu.roll(turned, edge_turn(x), 1)
            value = jnp.where(edge_lane[None], edge[0:ROWS].reshape(NV, WL, L), plane3(x))
            total = jnp.where(edge_lane, edge[ROWS:B1], rates[x, 0])
            rates[x, 0] = total
            rates[x, 1] = 1.0 / total
            for j in range(NV):
                ar[at(j, x), :] = value[j]
            store_split(x, value.reshape(ROWS, L), total)

    columns = jnp.zeros((B1, L), F32)
    for x in range(X):
        value = plane(x)
        store_split(x, value, one(R2, x))
        columns = collect(x, jnp.concatenate([value, one(R2, x)], axis=0), columns)
    put_columns(0, to_rows(columns))
    cols[0] = columns
    pack(0)
    pl.semaphore_wait(
        barrier,
        2
        + (st > 0).astype(jnp.int32)
        + (st < n_st - 1).astype(jnp.int32)
        + (wl > 0).astype(jnp.int32)
        + (wl < n_wl - 1).astype(jnp.int32),
    )
    send(0, far)
    send(0, near)

    @pl.when(at_wall)
    def _():
        for c in code_loads:
            c.wait()
        tg[...] = jnp.zeros((8, NV), F32)
        tg[0:4, :] = table[...]
        tg[4:5, :] = gain[...]
        own = (iota((ROWS, NV), 0) == WL * iota((ROWS, NV), 1)).astype(F32)
        hi, lo = split(tg[...])
        rest = (tg[...] - hi.astype(F32) - lo.astype(F32)).astype(BF)
        parts = jnp.concatenate([v.astype(F32) for v in (hi, lo, rest, jnp.zeros((8, NV), BF))], axis=0).astype(BF)
        coef = dot_nt(own.astype(BF), parts).astype(BF)

        def coef_of(p, _):
            hots = []
            for q in range(2):
                x = 2 * p + q
                codes = jnp.broadcast_to(code[pl.ds(x + off, 1), :], (8, L))
                spall = jnp.broadcast_to(mask[pl.ds(x + off, 1), :], (8, L))
                hot = jnp.where(sub < 4, (codes == sub).astype(F32), jnp.where(sub == 4, spall.astype(F32), 0.0))
                hots.append(jnp.concatenate([hot, hot, hot, jnp.zeros((8, L), F32)], axis=0))
            wall = dot(coef, jnp.concatenate(hots, axis=1).astype(BF))
            for q in range(2):
                x = 2 * p + q
                diag[:, x] = one(R1, x)[None] * wall[:, q * L : (q + 1) * L].reshape(NV, WL, L)
            return 0

        lax.fori_loop(0, PAIRS, coef_of, 0)

    loads[3].wait()
    local()
    receive(0, near)
    finish(0, False)
    receive(0, far)
    edge_adj = edges(0)
    put_columns(1, to_rows(edge_adj))
    send(1, far)
    apply(edge_adj)
    pack(1)
    send(1, near)
    local()
    receive(1, near)
    finish(1, True)
    receive(1, far)
    t_res[...], t_adj[...] = edges(1)
    for r in range(2):
        for n, c in enumerate(copies(r, range(6))):
            when(ways[n][1], c.wait_send)


def edge_turn(x):
    return (2 * L - 2 * x - 2) % L


def drain(adj, res, t_adj, t_res, adj_out, res_out, adj_buf, res_buf, sem):
    lane = iota((WL, L), 1)
    edge_lane = ((lane == 0) | (lane == L - 1))[None]
    copies = []
    for g, (low, high) in enumerate(((0, 2), (2, 5), (5, 9), (9, 13), (13, NV))):
        for n, (field, turned, buf, out) in enumerate(((adj, t_adj, adj_buf, adj_out), (res, t_res, res_buf, res_out))):
            part = pl.ds(low, high - low)
            for x in range(X):
                edge = pltpu.roll(turned[low * WL : high * WL, :], edge_turn(x), 1).reshape(high - low, WL, L)
                buf[low:high, x] = field[low:high, x] + jnp.where(edge_lane, edge, 0.0)
            copy = pltpu.make_async_copy(buf.at[part], out.at[part], sem.at[n, g])
            copy.start()
            copies.append(copy)
    for c in copies:
        c.wait()


def on_device(adj_init, adj_source, velocity, sound, face_couple, precond_inv, wall_code, spall_mask, wall_table, spall_gain):
    field = jax.ShapeDtypeStruct((NV, X, WL, L), F32)
    turned = jax.ShapeDtypeStruct((B1, L), F32)
    hbm = pl.BlockSpec(memory_space=pltpu.HBM)
    inside = pl.BlockSpec(memory_space=pltpu.VMEM)
    results = pl.pallas_call(
        kernel,
        out_shape=(field, field, turned, turned),
        in_specs=[hbm] * 10,
        out_specs=(inside,) * 4,
        scratch_shapes=[
            pltpu.VMEM((20 * X * WL, L), F32),
            pltpu.VMEM((NV, X, WL, L), F32),
            pltpu.VMEM((3, X, WL, L), F32),
            pltpu.VMEM((X, WL, L), F32),
            pltpu.VMEM((16, L), jnp.int32),
            pltpu.VMEM((16, L), jnp.int32),
            pltpu.VMEM((3, NV, 2, NV), F32),
            pltpu.VMEM((NV, NV), F32),
            pltpu.VMEM((4, NV), F32),
            pltpu.VMEM((1, NV), F32),
            pltpu.VMEM((NV, X, WL, L), F32),
            pltpu.VMEM((X, 2, B1, L), BF),
            pltpu.VMEM((PAIRS + 2, 6 * ROWS, 2 * L), F32),
            pltpu.VMEM((NV, X, WL, L), F32),
            pltpu.VMEM((6 * ROWS, 512), BF),
            pltpu.VMEM((B1, 512), BF),
            pltpu.VMEM((2 * B1, 768), BF),
            pltpu.VMEM((B1, 256), BF),
            pltpu.VMEM((8, NV), F32),
            pltpu.VMEM((2, 2, 18, WL, L), F32),
            pltpu.VMEM((2, 2, WROWS, L), F32),
            pltpu.VMEM((2, 2, 2, 16, L), F32),
            pltpu.VMEM((2, 2, 18, WL, L), F32),
            pltpu.VMEM((2, 2, 24 * X, L), F32),
            pltpu.VMEM((2, 2, 2, 16, L), F32),
            pltpu.VMEM((2, 32, L), F32),
            pltpu.VMEM((X, 4, WL, L), F32),
            pltpu.VMEM((2, B1, L), F32),
            pltpu.VMEM((2, WL, L), F32),
            pltpu.SemaphoreType.DMA((10,)),
            pltpu.SemaphoreType.DMA((2, 6)),
            pltpu.SemaphoreType.DMA((2, 6)),
        ],
        compiler_params=pltpu.CompilerParams(collective_id=0, has_side_effects=True, vmem_limit_bytes=40 * 1024 * 1024),
        name="sweeps",
    )(
        *[
            pltpu.with_memory_space_constraint(v, pltpu.HBM)
            for v in (
                adj_init.reshape(NV * X * WL, L),
                adj_source,
                velocity,
                sound,
                wall_code,
                spall_mask,
                face_couple.transpose(0, 2, 1, 3),
                precond_inv,
                wall_table,
                spall_gain.reshape(1, NV),
            )
        ]
    )
    return pl.pallas_call(
        drain,
        out_shape=(field, field),
        in_specs=[inside] * 4,
        out_specs=(hbm, hbm),
        scratch_shapes=[
            pltpu.VMEM((NV, X, WL, L), F32),
            pltpu.VMEM((NV, X, WL, L), F32),
            pltpu.SemaphoreType.DMA((2, PAIRS)),
        ],
        compiler_params=pltpu.CompilerParams(vmem_limit_bytes=40 * 1024 * 1024),
        name="drain",
    )(*results)


def solution(mesh):
    field = P(None, "stream", "wall", "span")
    return jax.shard_map(
        on_device,
        mesh=mesh,
        in_specs=(field, field, field, P("stream", "wall", "span"), P(), P(), P(), P(), P(), P()),
        out_specs=(field, field),
        check_vma=False,
    )
```

```python
import jax
import jax.numpy as jnp
from jax import lax
from jax.experimental import pallas as pl
from jax.experimental.pallas import tpu as pltpu
from jax.sharding import PartitionSpec as P

NV = 17
X = 12
WL = 8
L = 128
B1 = 144
ROWS = NV * WL
PAIRS = X // 2
R1, R0, R2 = 17, 18, 19
WROWS = 18 * X
F32, BF = jnp.float32, jnp.bfloat16
HI = lax.Precision.HIGHEST
MESH = pl.DeviceIdType.MESH


def iota(shape, dim):
    return lax.broadcasted_iota(jnp.int32, shape, dim)


def dot(a, b):
    return lax.dot_general(a, b, (((1,), (0,)), ((), ())), preferred_element_type=F32)


def dot_nt(a, b):
    return lax.dot_general(a, b, (((1,), (1,)), ((), ())), preferred_element_type=F32)


def split(v):
    hi = v.astype(BF)
    return hi, (v - hi.astype(F32)).astype(BF)


def stacked(hi, lo, rows):
    parts = [hi, lo, hi]
    short = rows - 3 * hi.shape[0]
    return jnp.concatenate(parts + [jnp.zeros((short, hi.shape[1]), BF)], axis=0)


def build_weights(fc, pinv, w_all, w_p, w_span, w_wall):
    spread = (iota((B1, NV), 0) // WL == iota((B1, NV), 1)).astype(BF)
    both = [jnp.concatenate(split(fc[d].reshape(2 * NV, NV)), axis=0) for d in range(3)]
    rows = [dot_nt(spread, v).astype(BF) for v in both]
    p_rows = jnp.concatenate([dot(spread, v).astype(BF) for v in split(pinv[...])], axis=1)

    def fold(k, length):
        return jnp.where(k >= 2 * length, k - 2 * length, jnp.where(k >= length, k - length, k))

    def picker(n_rows, width, length, s, low_at):
        js, k = iota((2 * n_rows, width), 0), iota((2 * n_rows, width), 1)
        low = js >= n_rows
        js = jnp.where(low, js - n_rows, js)
        kk = fold(k, length) if length else k
        if s is None:
            return js, k, kk, low == (k >= low_at)
        return js // 2, k, kk, (low == (k >= low_at)) & (js % 2 == s)

    k = iota((B1, 512), 1)
    w = iota((B1, 512), 0) % WL
    wk = fold(k, B1) % WL

    def expand(values, pick, shift):
        return jnp.where(wk == w + shift, dot(values, pick), 0.0)

    picks = []
    for s in range(2):
        j, kc, kk, ok = picker(2 * NV, 512, B1, s, 2 * B1)
        picks.append((ok & (kk // WL == j) & (kc < 3 * B1)).astype(BF))
    for d in range(3):
        shifts = (-1, 1) if d == 1 else (0, 0)
        pair = [expand(rows[d], picks[s], shifts[s])[:ROWS] for s in range(2)]
        w_all[2 * ROWS * d : 2 * ROWS * (d + 1), :] = jnp.concatenate(pair, axis=0).astype(BF)
    j, kc, kk, ok = picker(NV, 512, B1, None, 2 * B1)
    p_pick = (ok & (kk // WL == j) & (kc < 3 * B1)).astype(BF)
    w_p[...] = expand(p_rows, p_pick, 0).astype(BF)

    ks = iota((B1, 512), 1)
    rs = iota((B1, 512), 0)
    kq = jnp.where(ks >= 256, ks - 256, ks)
    same_cell = (rs % WL == kq % WL) & (kq < ROWS)

    for s in range(2):
        j, kc, _, ok = picker(2 * NV, 512, 0, s, 256)
        kk = jnp.where(kc >= 256, kc - 256, kc)
        full = dot(rows[2], (ok & (kk // WL == j)).astype(BF))
        full = jnp.where(same_cell, full, 0.0)
        full = jnp.where((rs >= ROWS) & (rs == ks), 1.0, full).astype(BF)
        w_span[B1 * s : B1 * (s + 1), 0:256] = full[:, 0:256]
        w_span[B1 * s : B1 * (s + 1), 256:768] = full

    ks, rs = iota((B1, 256), 1), iota((B1, 256), 0)
    full = 0.0
    for s in range(2):
        j, kc, kk, ok = picker(2 * NV, 256, 48, s, 96)
        part = dot(rows[1], (ok & (kk - 24 * s == j) & (kc < 144)).astype(BF))
        full = full + jnp.where(rs % WL == (WL - 1) * s, part, 0.0)
    w_wall[...] = jnp.where(rs < ROWS, full, 0.0).astype(BF)


def kernel(
    adj_in, src_in, vel_in, snd_in, code_in, mask_in, fc_in, pinv_in, table_in, gain_in,
    adj_out, res_out, t_adj, t_res,
    ar, src, vel, snd, code, mask, fc, pinv, table, gain, res, split_a, g_buf, diag,
    w_all, w_p, w_span, w_wall, tg,
    send_s, send_w, send_p, recv_s, recv_w, recv_p, spread, rates, cols, col_rates,
    in_sem, send_sem, recv_sem,
):
    st, sp, wl = (lax.axis_index(a) for a in ("stream", "span", "wall"))
    n_st, n_sp, n_wl = (lax.axis_size(a) for a in ("stream", "span", "wall"))
    right, left = lax.rem(sp + 1, n_sp), lax.rem(sp + n_sp - 1, n_sp)
    ways = [
        ({"stream": st + 1}, st < n_st - 1, st > 0),
        ({"stream": st - 1}, st > 0, st < n_st - 1),
        ({"wall": wl + 1}, wl < n_wl - 1, wl > 0),
        ({"wall": wl - 1}, wl > 0, wl < n_wl - 1),
        ({"span": right}, None, None),
        ({"span": left}, None, None),
    ]

    def when(cond, fn):
        if cond is None:
            fn()
        else:
            pl.when(cond)(fn)

    barrier = pltpu.get_barrier_semaphore()
    for device, sends, _ in ways[4:] + ways[:4]:
        when(sends, lambda device=device: pl.semaphore_signal(barrier, inc=1, device_id=device, device_id_type=MESH))

    loads = [
        pltpu.make_async_copy(adj_in, ar.at[0 : NV * X * WL, :], in_sem.at[0]),
        pltpu.make_async_copy(vel_in, vel, in_sem.at[1]),
        pltpu.make_async_copy(snd_in, snd, in_sem.at[2]),
        pltpu.make_async_copy(src_in, src, in_sem.at[3]),
    ]
    small = [
        pltpu.make_async_copy(fc_in, fc, in_sem.at[6]),
        pltpu.make_async_copy(pinv_in, pinv, in_sem.at[7]),
        pltpu.make_async_copy(table_in, table, in_sem.at[8]),
        pltpu.make_async_copy(gain_in, gain, in_sem.at[9]),
    ]
    for c in small + loads:
        c.start()
    row0 = pl.multiple_of(X * st - 4 * lax.rem(st, 2), 8)
    off = 4 * lax.rem(st, 2)
    col0 = pl.multiple_of(L * sp, L)
    at_wall = wl == 0
    code_loads = [
        pltpu.make_async_copy(code_in.at[pl.ds(row0, 16), pl.ds(col0, L)], code, in_sem.at[4]),
        pltpu.make_async_copy(mask_in.at[pl.ds(row0, 16), pl.ds(col0, L)], mask, in_sem.at[5]),
    ]

    @pl.when(at_wall)
    def _():
        for c in code_loads:
            c.start()

    for r in range(2):
        for side in range(2):
            recv_w[r, side, WROWS:, :] = jnp.zeros((recv_w.shape[2] - WROWS, L), F32)
            send_p[r, side] = jnp.zeros((2, 16, L), F32)

            @pl.when(jnp.logical_not(ways[side][2]))
            def _():
                recv_s[r, side] = jnp.zeros((18, WL, L), F32)

            @pl.when(jnp.logical_not(ways[2 + side][2]))
            def _():
                recv_w[r, side, 0:WROWS, :] = jnp.zeros((WROWS, L), F32)

    spread[...] = jnp.zeros((2, 32, L), F32)
    g_buf[0, 0:ROWS, :] = jnp.zeros((ROWS, 2 * L), F32)
    g_buf[PAIRS + 1, ROWS : 2 * ROWS, :] = jnp.zeros((ROWS, 2 * L), F32)
    for c in small:
        c.wait()
    build_weights(fc, pinv, w_all, w_p, w_span, w_wall)

    for c in loads[:3]:
        c.wait()
    for d, slot in ((0, R0), (1, R1), (2, R2)):
        ar[slot * X * WL : (slot + 1) * X * WL, :] = (jnp.abs(vel[d]) + snd[...]).reshape(X * WL, L)

    def at(slot, x):
        start = slot * X * WL + x * WL
        return pl.ds(start if isinstance(start, int) else pl.multiple_of(start, WL), WL)

    def one(slot, x):
        return ar[at(slot, x), :]

    def plane(x):
        return jnp.concatenate([one(j, x) for j in range(NV)], axis=0)

    def plane3(x):
        return plane(x).reshape(NV, WL, L)

    def store_split(x, value, extra):
        hi, lo = split(jnp.concatenate([value, extra], axis=0))
        split_a[x, 0] = hi
        split_a[x, 1] = lo

    def copies(r, which):
        out = []
        for n in which:
            device = ways[n][0]
            bufs = ((send_s, recv_s), (send_w, recv_w), (send_p, recv_p))[n // 2]
            side = n % 2
            if n // 2 == 1:
                dst = bufs[1].at[r, side, 0:WROWS, :]
            else:
                dst = bufs[1].at[r, side]
            out.append(
                pltpu.make_async_remote_copy(
                    src_ref=bufs[0].at[r, side],
                    dst_ref=dst,
                    send_sem=send_sem.at[r, n],
                    recv_sem=recv_sem.at[r, n],
                    device_id=device,
                    device_id_type=MESH,
                )
            )
        return out

    lanes3 = iota((B1, L), 1)
    pick_row, pick_col = iota((32, 2 * L), 0), iota((32, 2 * L), 1) % L
    pick_col = jnp.where(pick_row < 16, pick_col - 2 * pick_row - 1, pick_col - 2 * (pick_row - 16) - 2)
    pick_cols = ((pick_col == 0) & (pick_row % 16 < X)).astype(BF)

    def collect(x, value, into):
        moved = pltpu.roll(value, 2 * x + 2, 1)
        return jnp.where((lanes3 == 2 * x + 1) | (lanes3 == 2 * x + 2), moved, into)

    def to_rows(value):
        return dot_nt(pick_cols, jnp.concatenate(split(value), axis=1))

    def put_columns(r, value):
        for side in range(2):
            send_p[r, side, 0] = value[16 * side : 16 * side + 16, 0:L]
            send_p[r, side, 1, :, 0 : B1 - L] = value[16 * side : 16 * side + 16, L:B1]

    def pack_wall(r):
        for side, w in ((0, WL - 1), (1, 0)):
            send_w[r, side] = ar[pl.ds(w, WROWS, stride=WL), :]

    def pack_stream(r):
        for side, x in ((0, X - 1), (1, 0)):
            send_s[r, side, 0:NV] = plane3(x)
            send_s[r, side, NV] = one(R0, x)

    near, far = range(4), range(4, 6)

    def send(r, which):
        for n, c in zip(which, copies(r, which)):
            when(ways[n][1], c.start)

    def receive(r, which):
        for n, c in zip(which, copies(r, which)):
            when(ways[n][2], c.wait_recv)

    lane = iota((WL, L), 1)
    sub = iota((WL, L), 0)
    edge_lane = (lane == 0) | (lane == L - 1)

    def planes_rhs(hi_lo_pairs):
        return jnp.concatenate([stacked(h, l, 512) for h, l in hi_lo_pairs], axis=1)

    def local():
        def couple(p, _):
            rhs = planes_rhs([(split_a[2 * p + q, 0], split_a[2 * p + q, 1]) for q in range(2)])
            g_buf[p + 1] = dot(w_all[...], rhs)

        def gather(p, _):
            for q in range(2):
                x = 2 * p + q
                here = slice(q * L, (q + 1) * L)
                r0, r1, r2 = one(R0, x), one(R1, x), one(R2, x)
                m00 = 0.5 * (r0 + one(R0, max(x - 1, 0)))
                m01 = 0.5 * (r0 + one(R0, min(x + 1, X - 1)))
                m10 = 0.5 * (r1 + pltpu.roll(r1, 1, 0))
                m11 = 0.5 * (r1 + pltpu.roll(r1, WL - 1, 0))
                m20 = jnp.where(lane == 0, 0.0, 0.5 * (r2 + pltpu.roll(r2, 1, 1)))
                m21 = jnp.where(lane == L - 1, 0.0, 0.5 * (r2 + pltpu.roll(r2, L - 1, 1)))

                def g(page, n, part):
                    return g_buf[page, n * ROWS : (n + 1) * ROWS, part]

                lower, upper = slice(0, L), slice(L, 2 * L)
                g00 = g(p + 1, 0, lower) if q == 1 else g(p, 0, upper)
                g01 = g(p + 2, 1, lower) if q == 1 else g(p + 1, 1, upper)
                terms = [
                    (m00, g00),
                    (m01, g01),
                    (m10, g(p + 1, 2, here)),
                    (m11, g(p + 1, 3, here)),
                    (m20, pltpu.roll(g(p + 1, 4, here), 1, 1)),
                    (m21, pltpu.roll(g(p + 1, 5, here), L - 1, 1)),
                ]
                total = src[:, x]
                for m, v in terms:
                    total = total - m[None] * v.reshape(NV, WL, L)
                res[:, x] = total

        for p in range(PAIRS + 1):
            if p < PAIRS:
                couple(p, 0)
            if p > 0:
                gather(p - 1, 0)

        @pl.when(at_wall)
        def _():
            def wall_term(x, _):
                res[:, x] = res[:, x] - diag[:, x] * plane3(x)
                return 0

            lax.fori_loop(0, X, wall_term, 0)

    def finish(r, last):
        ends = [split(recv_s[r, side].reshape(B1, L)) for side in range(2)]
        g_ends = dot(w_all[0 : 2 * ROWS, :], planes_rhs(ends))
        for side, x in ((0, 0), (1, X - 1)):
            rate = 0.5 * (one(R0, x) + recv_s[r, side, NV])
            g_end = g_ends[side * ROWS : (side + 1) * ROWS, side * L : (side + 1) * L]
            res[:, x] = res[:, x] - rate[None] * g_end.reshape(NV, WL, L)

        columns = jnp.zeros((B1, L), F32)
        for p in range(PAIRS):
            xs = (2 * p, 2 * p + 1)
            rhs = []
            for x in xs:
                rows = jnp.concatenate([recv_w[r, side, pl.ds(x, 24, stride=X), :] for side in range(2)], axis=0)
                rhs.append(stacked(*split(rows), 256))
            g_wall = dot(w_wall[...], jnp.concatenate(rhs, axis=1))
            parts = []
            for q, x in enumerate(xs):
                if r == 0:
                    r0, r1, r2 = one(R0, x), one(R1, x), one(R2, x)
                    r0m = recv_s[r, 0, NV] if x == 0 else one(R0, x - 1)
                    r0p = recv_s[r, 1, NV] if x == X - 1 else one(R0, x + 1)
                    low = recv_w[r, 0, NV * X + x : NV * X + x + 1, :]
                    high = recv_w[r, 1, NV * X + x : NV * X + x + 1, :]
                    r1m = jnp.where(sub == 0, jnp.broadcast_to(low, (WL, L)), pltpu.roll(r1, 1, 0))
                    r1p = jnp.where(sub == WL - 1, jnp.broadcast_to(high, (WL, L)), pltpu.roll(r1, WL - 1, 0))
                    r2m = jnp.where(lane == 0, 0.0, pltpu.roll(r2, 1, 1))
                    r2p = jnp.where(lane == L - 1, 0.0, pltpu.roll(r2, L - 1, 1))
                    total = 1.0 + (r0 + r1 + r2) + 0.5 * ((r0m + r0p) + (r1m + r1p) + (r2m + r2p))
                    rates[x, 0] = total
                    rates[x, 1] = 1.0 / total
                    rates[x, 2] = jnp.where(sub == 0, 0.5 * (r1 + r1m), jnp.where(sub == WL - 1, 0.5 * (r1 + r1p), 0.0))
                total, rate_w = rates[x, 0], rates[x, 2]
                value = res[:, x] - total[None] * plane3(x)
                value = value - rate_w[None] * g_wall[0:ROWS, q * L : (q + 1) * L].reshape(NV, WL, L)
                if last:
                    res_out[:, x] = value
                value = jnp.concatenate([value.reshape(ROWS, L), jnp.zeros((WL, L), F32)], axis=0)
                parts.append(split(value))
            update = dot(w_p[...], planes_rhs(parts))
            for q, x in enumerate(xs):
                step = update[0:ROWS, q * L : (q + 1) * L].reshape(NV, WL, L)
                value = plane3(x) + step * rates[x, 1][None]
                if last:
                    adj_out[:, x] = value
                else:
                    for j in range(NV):
                        ar[at(j, x), :] = value[j]
                    step = jnp.concatenate([step.reshape(ROWS, L), rates[x, 0]], axis=0)
                    columns = collect(x, step, columns)
        if not last:
            cols[1] = columns

    def edges(r):
        for side in range(2):
            for half in range(2):
                spread[half, pl.ds(2 - side, X, stride=2), :] = recv_p[r, side, half, 0:X, :]
        hi, lo = split(jnp.concatenate([spread[0], spread[1]], axis=1))
        halo = jnp.concatenate([hi, lo, hi], axis=1)
        halo = jnp.concatenate([halo, jnp.zeros((L - 32, halo.shape[1]), BF)], axis=0)
        halo = dot_nt(w_span[...], halo)
        halo = jnp.where(lanes3 % 2 == 0, halo[0:B1], halo[B1 : 2 * B1])
        flow = halo[0:ROWS].reshape(NV, WL, L)
        if r == 0:
            beyond = halo[ROWS:B1]
            total = cols[1, ROWS:B1, :] + 0.5 * beyond
            rate = 0.5 * (cols[0, ROWS:B1, :] + beyond)
            used = (lane >= 1) & (lane <= 2 * X)
            total = jnp.where(used, total, 1.0)
            inverse = 1.0 / total
            col_rates[0] = rate
            col_rates[1] = inverse
            before = cols[0, 0:ROWS, :].reshape(NV, WL, L)
            change = -(0.5 * beyond)[None] * before - rate[None] * flow
        else:
            inverse = col_rates[1]
            change = -col_rates[0][None] * flow
        change = jnp.concatenate([change.reshape(ROWS, L), jnp.zeros((WL, L), F32)], axis=0)
        moved = dot(w_p[...], stacked(*split(change), 512))
        moved = moved[0:ROWS].reshape(NV, WL, L)
        if r == 0:
            update = cols[1, 0:ROWS, :].reshape(NV, WL, L) + moved
            value = before + update * inverse[None]
            return jnp.concatenate([value.reshape(ROWS, L), total], axis=0)
        return change, jnp.concatenate([(moved * inverse[None]).reshape(ROWS, L), jnp.zeros((WL, L), F32)], axis=0)

    def apply(turned, xs):
        for x in xs:
            edge = pltpu.roll(turned, edge_turn(x), 1)
            value = jnp.where(edge_lane[None], edge[0:ROWS].reshape(NV, WL, L), plane3(x))
            total = jnp.where(edge_lane, edge[ROWS:B1], rates[x, 0])
            rates[x, 0] = total
            rates[x, 1] = 1.0 / total
            for j in range(NV):
                ar[at(j, x), :] = value[j]
            store_split(x, value.reshape(ROWS, L), total)

    columns = jnp.zeros((B1, L), F32)
    for x in range(X):
        value = plane(x)
        store_split(x, value, one(R2, x))
        columns = collect(x, jnp.concatenate([value, one(R2, x)], axis=0), columns)
    put_columns(0, to_rows(columns))
    cols[0] = columns
    pack_stream(0)
    pack_wall(0)
    pl.semaphore_wait(
        barrier,
        2
        + (st > 0).astype(jnp.int32)
        + (st < n_st - 1).astype(jnp.int32)
        + (wl > 0).astype(jnp.int32)
        + (wl < n_wl - 1).astype(jnp.int32),
    )
    send(0, far)
    send(0, near)

    @pl.when(at_wall)
    def _():
        for c in code_loads:
            c.wait()
        tg[...] = jnp.zeros((8, NV), F32)
        tg[0:4, :] = table[...]
        tg[4:5, :] = gain[...]
        own = (iota((ROWS, NV), 0) == WL * iota((ROWS, NV), 1)).astype(F32)
        hi, lo = split(tg[...])
        rest = (tg[...] - hi.astype(F32) - lo.astype(F32)).astype(BF)
        parts = jnp.concatenate([v.astype(F32) for v in (hi, lo, rest, jnp.zeros((8, NV), BF))], axis=0).astype(BF)
        coef = dot_nt(own.astype(BF), parts).astype(BF)

        def coef_of(p, _):
            hots = []
            for q in range(2):
                x = 2 * p + q
                codes = jnp.broadcast_to(code[pl.ds(x + off, 1), :], (8, L))
                spall = jnp.broadcast_to(mask[pl.ds(x + off, 1), :], (8, L))
                hot = jnp.where(sub < 4, (codes == sub).astype(F32), jnp.where(sub == 4, spall.astype(F32), 0.0))
                hots.append(jnp.concatenate([hot, hot, hot, jnp.zeros((8, L), F32)], axis=0))
            wall = dot(coef, jnp.concatenate(hots, axis=1).astype(BF))
            for q in range(2):
                x = 2 * p + q
                diag[:, x] = one(R1, x)[None] * wall[:, q * L : (q + 1) * L].reshape(NV, WL, L)
            return 0

        lax.fori_loop(0, PAIRS, coef_of, 0)

    loads[3].wait()
    local()
    receive(0, near)
    finish(0, False)
    receive(0, far)
    edge_adj = edges(0)
    put_columns(1, to_rows(edge_adj))
    send(1, far)
    apply(edge_adj, (0, X - 1))
    pack_stream(1)
    send(1, range(2))
    apply(edge_adj, range(1, X - 1))
    pack_wall(1)
    send(1, range(2, 4))
    local()
    receive(1, near)
    finish(1, True)
    receive(1, far)
    t_res[...], t_adj[...] = edges(1)
    for r in range(2):
        for n, c in enumerate(copies(r, range(6))):
            when(ways[n][1], c.wait_send)


def edge_turn(x):
    return (2 * L - 2 * x - 2) % L


def drain(adj, res, t_adj, t_res, adj_out, res_out, adj_buf, res_buf, sem):
    lane = iota((WL, L), 1)
    edge_lane = ((lane == 0) | (lane == L - 1))[None]
    copies = []
    for g, (low, high) in enumerate(((0, 2), (2, 5), (5, 9), (9, 13), (13, NV))):
        for n, (field, turned, buf, out) in enumerate(((adj, t_adj, adj_buf, adj_out), (res, t_res, res_buf, res_out))):
            part = pl.ds(low, high - low)
            for x in range(X):
                edge = pltpu.roll(turned[low * WL : high * WL, :], edge_turn(x), 1).reshape(high - low, WL, L)
                buf[low:high, x] = field[low:high, x] + jnp.where(edge_lane, edge, 0.0)
            copy = pltpu.make_async_copy(buf.at[part], out.at[part], sem.at[n, g])
            copy.start()
            copies.append(copy)
    for c in copies:
        c.wait()


def on_device(adj_init, adj_source, velocity, sound, face_couple, precond_inv, wall_code, spall_mask, wall_table, spall_gain):
    field = jax.ShapeDtypeStruct((NV, X, WL, L), F32)
    turned = jax.ShapeDtypeStruct((B1, L), F32)
    hbm = pl.BlockSpec(memory_space=pltpu.HBM)
    inside = pl.BlockSpec(memory_space=pltpu.VMEM)
    results = pl.pallas_call(
        kernel,
        out_shape=(field, field, turned, turned),
        in_specs=[hbm] * 10,
        out_specs=(inside,) * 4,
        scratch_shapes=[
            pltpu.VMEM((20 * X * WL, L), F32),
            pltpu.VMEM((NV, X, WL, L), F32),
            pltpu.VMEM((3, X, WL, L), F32),
            pltpu.VMEM((X, WL, L), F32),
            pltpu.VMEM((16, L), jnp.int32),
            pltpu.VMEM((16, L), jnp.int32),
            pltpu.VMEM((3, NV, 2, NV), F32),
            pltpu.VMEM((NV, NV), F32),
            pltpu.VMEM((4, NV), F32),
            pltpu.VMEM((1, NV), F32),
            pltpu.VMEM((NV, X, WL, L), F32),
            pltpu.VMEM((X, 2, B1, L), BF),
            pltpu.VMEM((PAIRS + 2, 6 * ROWS, 2 * L), F32),
            pltpu.VMEM((NV, X, WL, L), F32),
            pltpu.VMEM((6 * ROWS, 512), BF),
            pltpu.VMEM((B1, 512), BF),
            pltpu.VMEM((2 * B1, 768), BF),
            pltpu.VMEM((B1, 256), BF),
            pltpu.VMEM((8, NV), F32),
            pltpu.VMEM((2, 2, 18, WL, L), F32),
            pltpu.VMEM((2, 2, WROWS, L), F32),
            pltpu.VMEM((2, 2, 2, 16, L), F32),
            pltpu.VMEM((2, 2, 18, WL, L), F32),
            pltpu.VMEM((2, 2, 24 * X, L), F32),
            pltpu.VMEM((2, 2, 2, 16, L), F32),
            pltpu.VMEM((2, 32, L), F32),
            pltpu.VMEM((X, 4, WL, L), F32),
            pltpu.VMEM((2, B1, L), F32),
            pltpu.VMEM((2, WL, L), F32),
            pltpu.SemaphoreType.DMA((10,)),
            pltpu.SemaphoreType.DMA((2, 6)),
            pltpu.SemaphoreType.DMA((2, 6)),
        ],
        compiler_params=pltpu.CompilerParams(collective_id=0, has_side_effects=True, vmem_limit_bytes=40 * 1024 * 1024),
        name="sweeps",
    )(
        *[
            pltpu.with_memory_space_constraint(v, pltpu.HBM)
            for v in (
                adj_init.reshape(NV * X * WL, L),
                adj_source,
                velocity,
                sound,
                wall_code,
                spall_mask,
                face_couple.transpose(0, 2, 1, 3),
                precond_inv,
                wall_table,
                spall_gain.reshape(1, NV),
            )
        ]
    )
    return pl.pallas_call(
        drain,
        out_shape=(field, field),
        in_specs=[inside] * 4,
        out_specs=(hbm, hbm),
        scratch_shapes=[
            pltpu.VMEM((NV, X, WL, L), F32),
            pltpu.VMEM((NV, X, WL, L), F32),
            pltpu.SemaphoreType.DMA((2, PAIRS)),
        ],
        compiler_params=pltpu.CompilerParams(vmem_limit_bytes=40 * 1024 * 1024),
        name="drain",
    )(*results)


def solution(mesh):
    field = P(None, "stream", "wall", "span")
    return jax.shard_map(
        on_device,
        mesh=mesh,
        in_specs=(field, field, field, P("stream", "wall", "span"), P(), P(), P(), P(), P(), P()),
        out_specs=(field, field),
        check_vma=False,
    )
```
